512 devices in a mesh: brow: 32 (over x, y, core), bcol: 16 (over z).
Axes of the slice: x: 4, y: 4, z: 16, core: 2. Of those that a mesh axis runs over, the one named last changes fastest.
Arguments:
- held_flow: float32 [19, 512, 16384], P(None, 'brow', 'bcol'), may hold values from 0.5 to 1.5
- held_heat: float32 [7, 512, 16384], P(None, 'brow', 'bcol'), may hold values from 0.5 to 1.5
- coarse_flow: bfloat16 [19, 32, 16, 4096], P(None, 'brow', 'bcol'), may hold values from 0.5 to 1.5
- coarse_heat: bfloat16 [7, 32, 16, 4096], P(None, 'brow', 'bcol'), may hold values from 0.5 to 1.5
- pair_mask: int32 [32], P('brow'), may hold values from 1 to 15, as said below
- moved_count: int32 [32, 16], P('brow', 'bcol'), may hold values from 0 to 1, as said below
- refine_src: int32 [32, 16, 4], P('brow', 'bcol'), may hold values from -1 to 255, as said below
Outputs:
- new_flow: float32 [19, 512, 16384], P(None, 'brow', 'bcol')
- new_heat: float32 [7, 512, 16384], P(None, 'brow', 'bcol')
The draws below stay inside these ranges and needn't reach their ends.
Inputs may be any that keep to these rules, and one draw needn't show every extreme that they name: `pair_mask`: every row of devices pairs columns by XOR with its own mask. `moved_count`: both devices of a pair hold the same count; some pair trades exactly 1 block in every draw. `refine_src`: each device has exactly 2 refined slots, of 2 different octants; for each block column and octant, no parent row is named by two devices of that column.
All inputs are finite; a program needn't handle non-finite values.
Results may differ from the reference program's by a relative error of at most 0.0013.
Values may be sent and summed in bfloat16 or wider, within the bound.
A program may use at most 128 MiB of HBM per device.

```python
import jax
import jax.numpy as jnp

BS = 16
KZ = 4
MMAX = 1
NX = 512
NY = 256
NZ = 64
CELLS = 4096
N_BROW = 32
N_BCOL = 16


def pairing(key):
    masks = jax.random.randint(jax.random.fold_in(key, 11), (N_BROW,), 1, N_BCOL).astype(jnp.int32)
    masks = masks.at[0].set(N_BCOL - 1)
    masks = masks.at[1].set(1)
    return masks


def draw_pair_mask(key, part):
    return pairing(key)


def draw_moved_count(key, part):
    masks = pairing(key)
    col_ids = jnp.arange(N_BCOL, dtype=jnp.int32)[None, :]
    row_ids = jnp.arange(N_BROW, dtype=jnp.int32)[:, None]
    lowest = jnp.minimum(col_ids, jnp.bitwise_xor(col_ids, masks[:, None]))
    table = jax.random.randint(jax.random.fold_in(key, 12), (N_BROW, N_BCOL), 0, MMAX + 1).astype(jnp.int32)
    counts = jnp.take_along_axis(table, lowest, axis=1)
    counts = jnp.where((row_ids == 0) & (lowest == 0), MMAX, counts)
    return counts.astype(jnp.int32)


def draw_refine_src(key, part):
    row_keys = jax.random.split(jax.random.fold_in(key, 21), N_BCOL * 8)
    perms = jax.vmap(lambda single: jax.random.permutation(single, N_BROW))(row_keys)
    perms = perms.reshape(N_BCOL, 8, N_BROW).astype(jnp.int32)
    corner = perms[0, 7, 0]
    col_ids = jnp.arange(N_BCOL, dtype=jnp.int32)[:, None, None]
    oct_ids = jnp.arange(8, dtype=jnp.int32)[None, :, None]
    rolled = (perms - corner + N_BROW - 1) % N_BROW
    perms = jnp.where((col_ids == 0) & (oct_ids == 7), rolled, perms).astype(jnp.int32)
    sources = perms.transpose(2, 0, 1)
    oct_keys = jax.random.split(jax.random.fold_in(key, 23), N_BROW * N_BCOL)
    octs = jax.vmap(lambda single: jax.random.permutation(single, 8))(oct_keys).reshape(N_BROW, N_BCOL, 8)[:, :, :2].astype(jnp.int32)
    dev_row = jnp.arange(N_BROW, dtype=jnp.int32)[:, None]
    dev_col = jnp.arange(N_BCOL, dtype=jnp.int32)[None, :]
    has_seven = jnp.any(octs == 7, axis=-1)
    first = jnp.where((dev_row == 0) & (dev_col == 0) & jnp.logical_not(has_seven), 7, octs[:, :, 0])
    octs = jnp.stack([first, octs[:, :, 1]], axis=-1).astype(jnp.int32)
    slot_keys = jax.random.split(jax.random.fold_in(key, 22), N_BROW * N_BCOL)
    slots = jax.vmap(lambda single: jax.random.permutation(single, KZ))(slot_keys).reshape(N_BROW, N_BCOL, KZ)
    rank_of = jnp.argsort(slots, axis=-1).astype(jnp.int32)
    octant_of = jnp.take_along_axis(octs, jnp.minimum(rank_of, 1), axis=-1)
    parent_row = jnp.take_along_axis(sources, octant_of, axis=-1)
    values = jnp.where(rank_of < 2, parent_row * 8 + octant_of, -1)
    return values.astype(jnp.int32)


def block_levels(stream_key, dims, cuts, low, top_value):
    factor_of = 1.0
    for dim, blocks in cuts:
        steps = jax.random.uniform(jax.random.fold_in(jax.random.fold_in(stream_key, 6), dim), (blocks,), jnp.float32, low / len(cuts), top_value / len(cuts))
        factor_of = factor_of * jnp.repeat(jnp.exp(steps), dims[dim] // blocks).reshape((-1,) + (1,) * (len(dims) - 1 - dim))
    return factor_of


def setup_inputs(seed: int = 0) -> dict:
    key_of = jax.random.split(jax.random.key(seed), 8)
    held_flow = jnp.clip(0.5 + 1.0 * jax.random.uniform(key_of[0], (19, NX, NY * NZ), jnp.float32) ** block_levels(key_of[0], (19, NX, NY * NZ), ((1, 32), (2, 16)), -0.2, 0.2), 0.5, 1.5)
    held_heat = jnp.clip(0.5 + 1.0 * jax.random.uniform(key_of[1], (7, NX, NY * NZ), jnp.float32) ** block_levels(key_of[1], (7, NX, NY * NZ), ((1, 32), (2, 16)), -0.2, 0.2), 0.5, 1.5)
    coarse_flow = jnp.clip(0.5 + 1.0 * jax.random.uniform(key_of[2], (19, N_BROW, N_BCOL, CELLS), jnp.float32) ** block_levels(key_of[2], (19, N_BROW, N_BCOL, CELLS), ((1, 32), (2, 16)), -0.2, 0.2), 0.5, 1.5).astype(jnp.bfloat16)
    coarse_heat = jnp.clip(0.5 + 1.0 * jax.random.uniform(key_of[3], (7, N_BROW, N_BCOL, CELLS), jnp.float32) ** block_levels(key_of[3], (7, N_BROW, N_BCOL, CELLS), ((1, 32), (2, 16)), -0.2, 0.2), 0.5, 1.5).astype(jnp.bfloat16)
    pair_mask = draw_pair_mask(jax.random.fold_in(key_of[7], 71), 0)
    moved_count = draw_moved_count(jax.random.fold_in(key_of[7], 71), 0)
    refine_src = draw_refine_src(jax.random.fold_in(key_of[7], 71), 0)
    return {"held_flow": held_flow, "held_heat": held_heat, "coarse_flow": coarse_flow, "coarse_heat": coarse_heat, "pair_mask": pair_mask, "moved_count": moved_count, "refine_src": refine_src}


flow_cx = [0, 1, -1, 0, 0, 0, 0, 1, -1, 1, -1, 1, -1, 1, -1, 0, 0, 0, 0]
flow_cy = [0, 0, 0, 1, -1, 0, 0, 1, -1, -1, 1, 0, 0, 0, 0, 1, -1, 1, -1]
flow_cz = [0, 0, 0, 0, 0, 1, -1, 0, 0, 0, 0, 1, -1, -1, 1, 1, -1, -1, 1]
flow_weight = [1.0 / 3.0] + [1.0 / 18.0] * 6 + [1.0 / 36.0] * 12
flow_reverse = [0, 2, 1, 4, 3, 6, 5, 8, 7, 10, 9, 12, 11, 14, 13, 16, 15, 18, 17]
heat_cx = [0, 1, -1, 0, 0, 0, 0]
heat_cy = [0, 0, 0, 1, -1, 0, 0]
heat_cz = [0, 0, 0, 0, 0, 1, -1]
heat_weight = [0.25] + [0.125] * 6
heat_reverse = [0, 2, 1, 4, 3, 6, 5]
tau_flow = 0.8
tau_heat = 0.7
tau_flow_coarse = 0.65
tau_heat_coarse = 0.6
buoyancy = 0.01
heat_ref = 7.0


def moments(lattice, forced):
    flow_pop = lattice[:19]
    heat_pop = lattice[19:]
    density = jnp.sum(flow_pop, axis=0)
    heat_value = jnp.sum(heat_pop, axis=0)
    mom_x = jnp.zeros_like(density)
    mom_y = jnp.zeros_like(density)
    mom_z = jnp.zeros_like(density)
    for channel in range(19):
        if flow_cx[channel] != 0:
            mom_x = mom_x + flow_cx[channel] * flow_pop[channel]
        if flow_cy[channel] != 0:
            mom_y = mom_y + flow_cy[channel] * flow_pop[channel]
        if flow_cz[channel] != 0:
            mom_z = mom_z + flow_cz[channel] * flow_pop[channel]
    push_up = jnp.zeros_like(density)
    if forced:
        push_up = buoyancy * density * (heat_value - heat_ref)
        mom_z = mom_z + 0.5 * push_up
    vel_x = mom_x / density
    vel_y = mom_y / density
    vel_z = mom_z / density
    return flow_pop, heat_pop, density, heat_value, push_up, vel_x, vel_y, vel_z


def equilibria(density, heat_value, vel_x, vel_y, vel_z):
    speed_sq = vel_x * vel_x + vel_y * vel_y + vel_z * vel_z
    flow_eq = []
    flow_dot = []
    for channel in range(19):
        along_dir = flow_cx[channel] * vel_x + flow_cy[channel] * vel_y + flow_cz[channel] * vel_z
        flow_dot.append(along_dir)
        flow_eq.append(flow_weight[channel] * density * (1.0 + 3.0 * along_dir + 4.5 * along_dir * along_dir - 1.5 * speed_sq))
    heat_eq = []
    for channel in range(7):
        along_dir = heat_cx[channel] * vel_x + heat_cy[channel] * vel_y + heat_cz[channel] * vel_z
        heat_eq.append(heat_weight[channel] * heat_value * (1.0 + 4.0 * along_dir))
    return flow_eq, flow_dot, heat_eq


def collide(lattice):
    flow_pop, heat_pop, density, heat_value, push_up, vel_x, vel_y, vel_z = moments(lattice, True)
    flow_eq, flow_dot, heat_eq = equilibria(density, heat_value, vel_x, vel_y, vel_z)
    new_rows = []
    for channel in range(19):
        source = (1.0 - 0.5 / tau_flow) * flow_weight[channel] * (3.0 * (flow_cz[channel] - vel_z) + 9.0 * flow_dot[channel] * flow_cz[channel]) * push_up
        new_rows.append(flow_pop[channel] - (flow_pop[channel] - flow_eq[channel]) / tau_flow + source)
    for channel in range(7):
        new_rows.append(heat_pop[channel] - (heat_pop[channel] - heat_eq[channel]) / tau_heat)
    return jnp.stack(new_rows, 0)


def explode(lattice):
    flow_pop, heat_pop, density, heat_value, push_up, vel_x, vel_y, vel_z = moments(lattice, False)
    flow_eq, flow_dot, heat_eq = equilibria(density, heat_value, vel_x, vel_y, vel_z)
    new_rows = []
    for channel in range(19):
        new_rows.append(flow_eq[channel] + (tau_flow / (2.0 * tau_flow_coarse)) * (flow_pop[channel] - flow_eq[channel]))
    for channel in range(7):
        new_rows.append(heat_eq[channel] + (tau_heat / (2.0 * tau_heat_coarse)) * (heat_pop[channel] - heat_eq[channel]))
    return jnp.stack(new_rows, 0)


def propagate(relaxed):
    width_x = relaxed.shape[1] - 2
    width_y = relaxed.shape[2] - 2
    new_rows = []
    for channel in range(26):
        if channel < 19:
            step_x, step_y, step_z = flow_cx[channel], flow_cy[channel], flow_cz[channel]
            reverse = flow_reverse[channel]
        else:
            step_x, step_y, step_z = heat_cx[channel - 19], heat_cy[channel - 19], heat_cz[channel - 19]
            reverse = 19 + heat_reverse[channel - 19]
        moved_in = relaxed[channel, 1 - step_x:1 - step_x + width_x, 1 - step_y:1 - step_y + width_y]
        bounce = relaxed[reverse, 1:1 + width_x, 1:1 + width_y]
        if step_z == 1:
            moved_in = jnp.concatenate([bounce[:, :, :1], moved_in[:, :, :-1]], axis=2)
        elif step_z == -1:
            moved_in = jnp.concatenate([moved_in[:, :, 1:], bounce[:, :, -1:]], axis=2)
        new_rows.append(moved_in)
    return jnp.stack(new_rows, 0)


def reference(held_flow, held_heat, coarse_flow, coarse_heat, pair_mask, moved_count, refine_src):
    half_edge = BS // 2
    held_all = jnp.concatenate([held_flow, held_heat], axis=0).reshape(26, NX, NY, NZ)
    blocked = held_all.reshape(26, N_BROW, BS, N_BCOL, BS, KZ, BS).transpose(0, 1, 3, 5, 2, 4, 6)
    row_ids = jnp.arange(N_BROW, dtype=jnp.int32)[:, None]
    col_ids = jnp.arange(N_BCOL, dtype=jnp.int32)[None, :]
    partner = jnp.bitwise_xor(col_ids, pair_mask[:, None])
    traded = blocked[:, row_ids, partner]
    slot_ids = jnp.arange(KZ, dtype=jnp.int32)
    migrate_here = slot_ids[None, None, :] < moved_count[:, :, None]
    lattice = jnp.where(migrate_here[None, :, :, :, None, None, None], traded, blocked)
    coarse_all = jnp.concatenate([coarse_flow, coarse_heat], axis=0).astype(jnp.float32)
    fine_cells = explode(coarse_all).reshape(26, N_BROW, N_BCOL, 2, half_edge, 2, half_edge, 2, half_edge)
    fine_cells = fine_cells.transpose(0, 1, 2, 3, 5, 7, 4, 6, 8).reshape(26, N_BROW, N_BCOL, 8, half_edge, half_edge, half_edge)
    usable = jnp.maximum(refine_src, 0)
    parent_row = usable // 8
    octant = usable % 8
    picked = fine_cells[:, parent_row, col_ids[:, :, None], octant]
    picked = jnp.repeat(jnp.repeat(jnp.repeat(picked, 2, axis=4), 2, axis=5), 2, axis=6)
    lattice = jnp.where((refine_src >= 0)[None, :, :, :, None, None, None], picked, lattice)
    lattice = lattice.transpose(0, 1, 4, 2, 5, 3, 6).reshape(26, BS * N_BROW, BS * N_BCOL, KZ * BS)
    for substep in range(2):
        relaxed = collide(lattice)
        padded = jnp.pad(relaxed, ((0, 0), (1, 1), (1, 1), (0, 0)), mode="wrap")
        lattice = propagate(padded)
    lattice = lattice.reshape(26, NX, NY * NZ)
    return lattice[:19], lattice[19:]
```

```python
import jax
import jax.numpy as jnp
import numpy as np
from jax import lax
from jax.experimental import pallas as pl
from jax.experimental.pallas import tpu as pltpu
from jax.sharding import PartitionSpec as P

MESH = pl.DeviceIdType.MESH
F32 = jnp.float32
BF16 = jnp.bfloat16

NPOP = 26
LX = 16
LANES = 1024
RING = 16
STEPS = 8
SPLITS = ((0, 9), (9, 18), (18, 26))
ROWS_A, ROWS_B = 64, 48

flow_cx = [0, 1, -1, 0, 0, 0, 0, 1, -1, 1, -1, 1, -1, 1, -1, 0, 0, 0, 0]
flow_cy = [0, 0, 0, 1, -1, 0, 0, 1, -1, -1, 1, 0, 0, 0, 0, 1, -1, 1, -1]
flow_cz = [0, 0, 0, 0, 0, 1, -1, 0, 0, 0, 0, 1, -1, -1, 1, 1, -1, -1, 1]
flow_weight = [1.0 / 3.0] + [1.0 / 18.0] * 6 + [1.0 / 36.0] * 12
flow_reverse = [0, 2, 1, 4, 3, 6, 5, 8, 7, 10, 9, 12, 11, 14, 13, 16, 15, 18, 17]
heat_reverse = [0, 2, 1, 4, 3, 6, 5]
POP_CX = flow_cx + flow_cx[:7]
POP_CY = flow_cy + flow_cy[:7]
POP_CZ = flow_cz + flow_cz[:7]
POP_REV = flow_reverse + [19 + r for r in heat_reverse]
X_UP = [i for i in range(NPOP) if POP_CX[i] == 1]
X_DOWN = [i for i in range(NPOP) if POP_CX[i] == -1]
Y_UP = [i for i in range(NPOP) if POP_CY[i] == 1]
Y_DOWN = [i for i in range(NPOP) if POP_CY[i] == -1]
CORNERS = ((7, 1, 1), (8, -1, -1), (9, 1, -1), (10, -1, 1))
tau_flow = 0.8
tau_heat = 0.7
tau_flow_coarse = 0.65
tau_heat_coarse = 0.6
buoyancy = 0.01
heat_ref = 7.0


def ring_seats(mask):
    packets = []
    for c in range(RING):
        d = ((c ^ mask) - c) % RING
        if d < STEPS:
            packets += [(d, c, 0), (d, c, 1)]
        elif d == STEPS:
            packets += [(d, c, 0)]
    packets.sort(key=lambda p: (-p[0], p[1], p[2]))
    busy = {}
    out = {}

    def place(n):
        if n == len(packets):
            return True
        d, c, h = packets[n]
        first = out[(c, 0)] + 1 if h == 1 else 0
        for t0 in range(first, STEPS - d + 1):
            taken = busy.setdefault((c - t0) % RING, [])
            if all(t0 + d <= a or b <= t0 for a, b in taken):
                taken.append((t0, t0 + d))
                out[(c, h)] = t0
                if place(n + 1):
                    return True
                taken.pop()
                del out[(c, h)]
        return False

    assert place(0)
    return out


def ring_tables():
    send = np.zeros((RING, RING, 2, STEPS), np.int64)
    land = np.zeros((RING, RING, 2), np.int64)
    send[:, :, :, 0] = 1
    for mask in range(1, RING):
        up = ring_seats(mask)
        for (c, h), t0 in up.items():
            d = ((c ^ mask) - c) % RING
            send[mask, c, 0, t0] = 1 + h
            land[mask, c ^ mask, h] = t0 + d - 1
            mc = RING - 1 - c
            mh = 1 if d == STEPS else h
            send[mask, mc, 1, t0] = 1 + mh
            land[mask, mc ^ mask, mh] = STEPS + t0 + d - 1
    word = np.zeros((RING, RING), np.int64)
    for t in range(STEPS):
        word |= send[:, :, 0, t] << (2 * t)
        word |= send[:, :, 1, t] << (16 + 2 * t)
    word = np.where(word >= 2**31, word - 2**32, word).astype(np.int32)
    return np.stack([word.reshape(-1), land[:, :, 0].reshape(-1).astype(np.int32),
                     land[:, :, 1].reshape(-1).astype(np.int32)])


RING_TABLE = ring_tables()


def lane_ids(rows):
    return lax.broadcasted_iota(jnp.int32, (rows, 128), 1)


def total(values):
    values = list(values)
    while len(values) > 1:
        values = [a + b for a, b in zip(values[::2], values[1::2])] + (
            [values[-1]] if len(values) % 2 else [])
    return values[0]


def moments(f, push):
    rho = total(f[:19])
    heat = total(f[19:])

    def along(c):
        ups = [f[i] for i in range(19) if c[i] == 1]
        downs = [f[i] for i in range(19) if c[i] == -1]
        return total([u - d for u, d in zip(ups, downs)])

    mx, my, mz = along(flow_cx), along(flow_cy), along(flow_cz)
    force = None
    if push:
        force = buoyancy * rho * (heat - heat_ref)
        mz = mz + 0.5 * force
    inv = 1.0 / rho
    return rho, heat, force, (mx, my, mz), (mx * inv, my * inv, mz * inv)


def dot_dir(i, v):
    terms = []
    for c, a in zip((flow_cx[i], flow_cy[i], flow_cz[i]), v):
        if c:
            terms.append((c, a))
    out = terms[0][1] if terms[0][0] > 0 else -terms[0][1]
    for c, a in terms[1:]:
        out = out + a if c > 0 else out - a
    return out


PAIRS = [(1, 2), (3, 4), (5, 6), (7, 8), (9, 10), (11, 12), (13, 14), (15, 16), (17, 18)]


def collide(f):
    rho, heat, force, mom, vel = moments(f, True)
    rate = 1.0 / tau_flow
    keep = 1.0 - rate
    gain = 1.0 - 0.5 / tau_flow
    speed = mom[0] * vel[0] + mom[1] * vel[1] + mom[2] * vel[2]
    common = rate * rho - (1.5 * rate) * speed - (3.0 * gain) * force * vel[2]
    fgain = (9.0 * gain) * force
    fodd = (3.0 * gain) * force
    out = [None] * NPOP
    out[0] = keep * f[0] + flow_weight[0] * common
    for i, j in PAIRS:
        w = flow_weight[i]
        cu = dot_dir(i, vel)
        cm = dot_dir(i, mom)
        bracket = (4.5 * rate) * cm
        odd = (3.0 * rate) * cm
        if flow_cz[i] == 1:
            bracket = bracket + fgain
            odd = odd + fodd
        elif flow_cz[i] == -1:
            bracket = bracket - fgain
            odd = odd - fodd
        even = common + bracket * cu
        out[i] = keep * f[i] + w * (even + odd)
        out[j] = keep * f[j] + w * (even - odd)
    hrate = 1.0 / tau_heat
    hkeep = 1.0 - hrate
    out[19] = hkeep * f[19] + (0.25 * hrate) * heat
    side = (0.125 * hrate) * heat
    for k, a in zip((20, 22, 24), vel):
        tilt = 4.0 * side * a
        out[k] = hkeep * f[k] + (side + tilt)
        out[k + 1] = hkeep * f[k + 1] + (side - tilt)
    return out


def explode(f):
    rho, heat, _, mom, vel = moments(f, False)
    blend = tau_flow / (2.0 * tau_flow_coarse)
    rest = 1.0 - blend
    speed = mom[0] * vel[0] + mom[1] * vel[1] + mom[2] * vel[2]
    common = rest * rho - (1.5 * rest) * speed
    out = [None] * NPOP
    out[0] = blend * f[0] + flow_weight[0] * common
    for i, j in PAIRS:
        w = flow_weight[i]
        cu = dot_dir(i, vel)
        cm = dot_dir(i, mom)
        even = common + ((4.5 * rest) * cm) * cu
        odd = (3.0 * rest) * cm
        out[i] = blend * f[i] + w * (even + odd)
        out[j] = blend * f[j] + w * (even - odd)
    hblend = tau_heat / (2.0 * tau_heat_coarse)
    hrest = 1.0 - hblend
    out[19] = hblend * f[19] + (0.25 * hrest) * heat
    side = (0.125 * hrest) * heat
    for k, a in zip((20, 22, 24), vel):
        tilt = 4.0 * side * a
        out[k] = hblend * f[k] + (side + tilt)
        out[k + 1] = hblend * f[k + 1] + (side - tilt)
    return out


def held_tile(hf, hh, p, rows, cols):
    return hf[p, rows, cols] if p < 19 else hh[p - 19, rows, cols]


def pack_trade(hf, hh, own):
    group = lane_ids(LX) % 64 // 16
    for p in range(NPOP):
        for q in range(2):
            packed = None
            for kk in range(4):
                k = 4 * q + kk
                tile = held_tile(hf, hh, p, slice(None), slice(128 * k, 128 * k + 128))
                if kk == 0:
                    packed = tile
                else:
                    packed = jnp.where(group == kk, pltpu.roll(tile, 16 * kk, 1), packed)
            own[q, p] = packed.astype(BF16)


def pack_coarse(cf, ch, spread, put):
    for t in range(32):
        cols = slice(128 * t, 128 * t + 128)
        flow = cf[:, cols].astype(F32)
        heat = ch[:, cols].astype(F32)
        spread[pl.ds(t, 8, stride=32), :] = flow[0:8]
        spread[pl.ds(8 * 32 + t, 8, stride=32), :] = flow[8:16]
        spread[pl.ds(16 * 32 + t, 3, stride=32), :] = flow[16:19]
        spread[pl.ds(19 * 32 + t, 7, stride=32), :] = heat
    high = lane_ids(8) // 8 % 2 == 1
    zeros = jnp.zeros((8, 128), F32)
    for ox in range(2):
        for oy in range(2):
            low_rows, high_rows = [], []
            for pair in range(13):
                a = spread[pl.ds(pair * 32 + 16 * ox + oy, 8, stride=2), :]
                b = spread[pl.ds((pair + 13) * 32 + 16 * ox + oy, 8, stride=2), :]
                low_rows.append(jnp.where(high, pltpu.roll(b, 8, 1), a))
                high_rows.append(jnp.where(high, b, pltpu.roll(a, 120, 1)))
            for oz, rows in ((0, low_rows), (1, high_rows)):
                rows = rows + [zeros]
                for i in range(7):
                    put(4 * ox + 2 * oy + oz, i,
                        jnp.concatenate([rows[2 * i], rows[2 * i + 1]], axis=0).astype(BF16))


def pack_kernel(hf, hh, cf, ch, own, part_a, part_b, spread):
    pack_trade(hf, hh, own)

    def put(octant, i, value):
        if i < 4:
            part_a[octant, 16 * i:16 * i + 16, :] = value
        else:
            part_b[octant, 16 * (i - 4):16 * (i - 4) + 16, :] = value

    pack_coarse(cf, ch, spread, put)


def place():
    me = lax.axis_index("brow")
    col = lax.axis_index("bcol")
    return me // 8, me // 2 % 4, me % 2, col


def row_of(x, y, k):
    return (x * 4 + y) * 2 + k


OFFSETS = [(d, dk) for d in range(4) for dk in range(2)]


def blocks_kernel(table, mask_ref, codes_in, own, part_a, part_b,
                  arrived, picked_a, picked_b,
                  landing, leaving, held_a, held_b, codes, stage_a, stage_b, got_a, got_b,
                  ring_send, ring_recv, code_send, code_recv, one_send, one_recv,
                  two_send, two_recv):
    x, y, k, col = place()
    me = row_of(x, y, k)
    cols = ((col + 1) % RING, (col + RING - 1) % RING)
    x_group = [row_of(x, (y + d) % 4, (k + dk) % 2) for d, dk in OFFSETS]
    y_group = [row_of((x + d) % 4, y, (k + dk) % 2) for d, dk in OFFSETS]
    peers = x_group[1:] + y_group[2:]

    barrier = pltpu.get_barrier_semaphore()
    for c in cols:
        pl.semaphore_signal(barrier, inc=1, device_id=(me, c), device_id_type=MESH)
    for peer in peers:
        pl.semaphore_signal(barrier, inc=1, device_id=(peer, col), device_id_type=MESH)
    pl.semaphore_wait(barrier, 2 + len(peers))

    pending = []

    def send(source, target, sends, recvs, device):
        copy = pltpu.make_async_remote_copy(
            src_ref=source, dst_ref=target, send_sem=sends, recv_sem=recvs,
            device_id=device, device_id_type=MESH)
        copy.start()
        pending.append(copy)
        return copy

    entry = mask_ref[0] * RING + col
    word = table[0, entry]
    ring = {}

    def ring_step(step):
        for s, (lo, hi) in enumerate(SPLITS):
            for way in range(2):
                code = (word >> (16 * way + 2 * step)) & 3
                other = own[0, lo:hi]
                if step:
                    ring[way, step - 1, s].wait_recv()
                    other = jnp.where(code == 1, other, landing[way * STEPS + step - 1, lo:hi])
                slot = way * STEPS + step
                leaving[slot, lo:hi] = jnp.where(code == 2, own[1, lo:hi], other)
                ring[way, step, s] = send(
                    leaving.at[slot, lo:hi], landing.at[slot, lo:hi],
                    ring_send.at[slot, s], ring_recv.at[slot, s], (me, cols[way]))

    ring_step(0)
    code_copies = [send(codes_in, codes.at[n], code_send.at[n], code_recv.at[n], (peer, col))
                   for n, peer in enumerate(peers)]
    one_copies = []
    for d in (2, 1, 3):
        one_copies.append(send(part_a, held_a.at[d], one_send.at[0, d], one_recv.at[0, d],
                               (x_group_of(x, y, k, d), col)))
        one_copies.append(send(part_b, held_b.at[d], one_send.at[1, d], one_recv.at[1, d],
                               (row_of(x, (y + d) % 4, k), col)))
    held_a[0] = part_a[...]
    held_b[0] = part_b[...]
    ring_step(1)
    ring_step(2)
    ring_step(3)

    for copy in code_copies + one_copies:
        copy.wait_recv()

    def wanted(n):
        values = [codes_in[0, 0, j] if n is None else codes[n, 0, 0, j] for j in range(4)]
        first = values[3]
        last = values[0]
        for j in (2, 1, 0):
            first = jnp.where(values[j] >= 0, values[j], first)
        for j in (1, 2, 3):
            last = jnp.where(values[j] >= 0, values[j], last)
        return first, last

    mine = wanted(None)
    two_copies = []
    for n, (d, dk) in enumerate(OFFSETS):
        for part, (group, stage, got, held, home) in enumerate((
                (x_group, stage_a, got_a, held_a, x), (y_group, stage_b, got_b, held_b, y))):
            if n == 0:
                pair = mine
            else:
                back = OFFSETS.index(((4 - d) % 4, dk))
                pair = wanted(back - 1 if part == 0 or d == 0 else 7 + back - 2)
            for s, code in enumerate(pair):
                parent = (code >> 6) & 3 if part == 0 else (code >> 4) & 3
                value = held[(home - parent + 4) & 3, code & 7]
                if n == 0:
                    got[0, s] = value
                else:
                    stage[n, s] = value
            if n:
                two_copies.append(send(stage.at[n], got.at[n], two_send.at[part, n],
                                       two_recv.at[part, n], (group[n], col)))
    for step in range(4, STEPS):
        ring_step(step)

    for copy in two_copies:
        copy.wait_recv()
    for s, code in enumerate(mine):
        core = ((code >> 3) & 1) ^ k
        picked_a[s] = got_a[((y - ((code >> 4) & 3) + 4) & 3) * 2 + core, s]
        picked_b[s] = got_b[((x - ((code >> 6) & 3) + 4) & 3) * 2 + core, s]
    for way in range(2):
        for s in range(len(SPLITS)):
            ring[way, STEPS - 1, s].wait_recv()
    for h in range(2):
        arrived[h] = landing[table[1 + h, entry]]
    for copy in pending:
        copy.wait_send()


def x_group_of(x, y, k, d):
    return row_of((x + d) % 4, y, k)


def edge_faces(field, xs, ys, cs, base, lead):
    low = lane_ids(LX) < 64
    for n, p in enumerate(X_UP):
        xs[0, n:n + 1, :] = field[p, base + 15:base + 16, lead:lead + LANES]
    for n, p in enumerate(X_DOWN):
        xs[1, n:n + 1, :] = field[p, base:base + 1, lead:lead + LANES]
    rows = slice(base, base + LX)
    last = slice(lead + LANES - 128, lead + LANES)
    first = slice(lead, lead + 128)
    for n in range(3):
        a, b = Y_UP[2 * n], Y_UP[2 * n + 1]
        ys[0, n] = jnp.where(low, pltpu.roll(field[a, rows, last], 64, 1), field[b, rows, last])
        a, b = Y_DOWN[2 * n], Y_DOWN[2 * n + 1]
        ys[1, n] = jnp.where(low, field[a, rows, first], pltpu.roll(field[b, rows, first], 64, 1))
    for n, (p, sx, sy) in enumerate(CORNERS):
        cs[n] = field[p, base + 8:base + 16, last] if (sx, sy) == (1, 1) else (
            field[p, base:base + 8, first] if (sx, sy) == (-1, -1) else (
                field[p, base + 8:base + 16, first] if (sx, sy) == (1, -1) else
                field[p, base:base + 8, last]))


def widen(relaxed, xr, yr, cr, wide):
    for p in range(NPOP):
        wide[p, 8:24, 128:128 + LANES] = relaxed[p]
    fill_edges(xr, yr, cr, wide)


def fill_edges(xr, yr, cr, wide):
    for n, (p, sx, sy) in enumerate(CORNERS):
        rows = slice(0, 8) if sx == 1 else slice(24, 32)
        cols = slice(0, 128) if sy == 1 else slice(128 + LANES, 256 + LANES)
        wide[p, rows, cols] = cr[n]
    for n, p in enumerate(X_UP):
        wide[p, 7:8, 128:128 + LANES] = xr[0, n:n + 1, :]
    for n, p in enumerate(X_DOWN):
        wide[p, 24:25, 128:128 + LANES] = xr[1, n:n + 1, :]
    for n in range(3):
        a, b = Y_UP[2 * n], Y_UP[2 * n + 1]
        wide[a, 8:24, 0:128] = pltpu.roll(yr[0, n], 64, 1)
        wide[b, 8:24, 0:128] = yr[0, n]
        a, b = Y_DOWN[2 * n], Y_DOWN[2 * n + 1]
        wide[a, 8:24, 128 + LANES:256 + LANES] = yr[1, n]
        wide[b, 8:24, 128 + LANES:256 + LANES] = pltpu.roll(yr[1, n], 64, 1)


def pulled(wide, p, rt, k):
    cx, cy, cz = POP_CX[p], POP_CY[p], POP_CZ[p]
    rows = slice(8 + 8 * rt - cx, 16 + 8 * rt - cx)

    def tile(e):
        return pl.ds(pl.multiple_of(128 * e, 128), 128)

    low = lane_ids(8) < 64
    value = wide[p, rows, tile(k + 1)]
    shift = 0
    if cy == 1:
        value = jnp.where(low, value, wide[p, rows, tile(k)])
        shift = 64
    elif cy == -1:
        value = jnp.where(low, wide[p, rows, tile(k + 2)], value)
        shift = 64
    shift = (shift + cz) % 128
    if shift:
        value = pltpu.roll(value, shift, 1)
    if cz:
        wall = lane_ids(8) % 64 == (0 if cz == 1 else 63)
        back = wide[POP_REV[p], 8 + 8 * rt:16 + 8 * rt, tile(k + 1)]
        value = jnp.where(wall, back, value)
    return value


def start_kernel(codes_in, moved, hf, hh, arrived, picked_a, picked_b,
                 relaxed, xs, ys, cs, spread, left, right, fresh):
    high = lane_ids(8) // 8 % 2 == 1
    values = [None] * NPOP
    for pair in range(13):
        part, row = (picked_a, 8 * pair) if pair < 8 else (picked_b, 8 * pair - 64)
        base = row // 16 * 16
        a = part[0, base:base + 16, :].astype(F32)[row - base:row - base + 8]
        b = part[1, base:base + 16, :].astype(F32)[row - base:row - base + 8]
        values[pair] = jnp.where(high, pltpu.roll(b, 8, 1), a)
        values[pair + 13] = jnp.where(high, b, pltpu.roll(a, 120, 1))
    for p, value in enumerate(explode(values)):
        spread[pl.ds(16 * p, 8, stride=2), :] = value
        spread[pl.ds(16 * p + 1, 8, stride=2), :] = value
    for p in range(NPOP):
        rows = slice(16 * p, 16 * p + 16)
        value = spread[rows, :]
        top = value.astype(BF16)
        left[rows, 0:128] = top
        left[rows, 128:256] = (value - top.astype(F32)).astype(BF16)
        left[rows, 256:384] = arrived[0, p]
        left[rows, 384:512] = arrived[1, p]

    source = [codes_in[0, 0, j] for j in range(4)]
    refined = [jnp.where(v >= 0, 1, 0) for v in source]
    rank = [0]
    for j in range(3):
        rank.append(rank[-1] + refined[j])
    child = [jnp.where(refined[j] == 1, rank[j] * 8, 1 << 20) for j in range(4)]
    trade = jnp.where((moved[0, 0] > 0) & (refined[0] == 0), 0, 1 << 20)

    def by_slot(lane, picks):
        slot = lane % 64 // 16
        return jnp.where(slot == 0, picks[0], jnp.where(
            slot == 1, picks[1], jnp.where(slot == 2, picks[2], picks[3])))

    for t in range(8):
        lane = lax.broadcasted_iota(jnp.int32, (1, 128), 1)
        yy = 2 * t + lane // 64
        want = yy // 2 * 16 + lane % 16 // 2 + by_slot(lane, child)
        row = lax.broadcasted_iota(jnp.int32, (128, 128), 0)
        hot = jnp.where(row == want, 1.0, 0.0).astype(BF16)
        cols = slice(128 * t, 128 * t + 128)
        right[0:128, cols] = hot
        right[128:256, cols] = hot
        row = lax.broadcasted_iota(jnp.int32, (256, 128), 0)
        z = lane % 64
        want = yy // 8 * 128 + yy % 2 * 64 + yy % 8 // 2 * 16 + z
        want = jnp.where(z < 16, want + trade, 1 << 20)
        right[256:512, cols] = jnp.where(row == want, 1.0, 0.0).astype(BF16)
    for t in range(4):
        cols = slice(256 * t, 256 * t + 256)
        fresh[:, cols] = jnp.dot(left[...], right[:, cols], preferred_element_type=F32)

    keep = [jnp.where(refined[j] == 1, 0, 1) for j in range(4)]
    keep[0] = jnp.where(moved[0, 0] > 0, 0, keep[0])
    kept = by_slot(lane_ids(8), keep) == 1

    def body(k, carry):
        cols = pl.ds(pl.multiple_of(128 * k, 128), 128)
        for rt in range(2):
            rows = slice(8 * rt, 8 * rt + 8)
            f = [jnp.where(kept, held_tile(hf, hh, p, rows, cols),
                           fresh[16 * p + 8 * rt:16 * p + 8 * rt + 8, cols])
                 for p in range(NPOP)]
            for p, value in enumerate(collide(f)):
                relaxed[p, rows, cols] = value
        return carry

    lax.fori_loop(0, 8, body, 0)
    edge_faces(relaxed, xs, ys, cs, 0, 0)


def step_kernel(relaxed_in, xr, yr, cr, relaxed, xs, ys, cs, wide):
    widen(relaxed_in, xr, yr, cr, wide)

    def body(k, carry):
        cols = pl.ds(pl.multiple_of(128 * k, 128), 128)
        for rt in range(2):
            f = [pulled(wide, p, rt, k) for p in range(NPOP)]
            for p, value in enumerate(collide(f)):
                relaxed[p, 8 * rt:8 * rt + 8, cols] = value
        return carry

    lax.fori_loop(0, 8, body, 0)
    edge_faces(relaxed, xs, ys, cs, 0, 0)


def final_kernel(relaxed_in, xr, yr, cr, out_flow, out_heat, wide):
    widen(relaxed_in, xr, yr, cr, wide)

    def body(k, carry):
        cols = pl.ds(pl.multiple_of(128 * k, 128), 128)
        for rt in range(2):
            for p in range(NPOP):
                value = pulled(wide, p, rt, k)
                if p < 19:
                    out_flow[p, 8 * rt:8 * rt + 8, cols] = value
                else:
                    out_heat[p - 19, 8 * rt:8 * rt + 8, cols] = value
        return carry

    lax.fori_loop(0, 8, body, 0)


def halo_kernel(xs, ys, cs, xr, yr, cr, send_sem, recv_sem):
    row = lax.axis_index("brow")
    col = lax.axis_index("bcol")
    rows = {1: (row + 1) % 32, -1: (row + 31) % 32, 0: row}
    cols = {1: (col + 1) % RING, -1: (col + RING - 1) % RING, 0: col}
    moves = [(xs.at[0], xr.at[0], 1, 0), (xs.at[1], xr.at[1], -1, 0),
             (ys.at[0], yr.at[0], 0, 1), (ys.at[1], yr.at[1], 0, -1)]
    for n, (p, sx, sy) in enumerate(CORNERS):
        moves.append((cs.at[n], cr.at[n], sx, sy))
    barrier = pltpu.get_barrier_semaphore()
    for _, _, sx, sy in moves:
        pl.semaphore_signal(barrier, inc=1, device_id=(rows[sx], cols[sy]), device_id_type=MESH)
    pl.semaphore_wait(barrier, len(moves))
    copies = []
    for n, (source, target, sx, sy) in enumerate(moves):
        copy = pltpu.make_async_remote_copy(
            src_ref=source, dst_ref=target, send_sem=send_sem.at[n], recv_sem=recv_sem.at[n],
            device_id=(rows[sx], cols[sy]), device_id_type=MESH)
        copy.start()
        copies.append(copy)
    for copy in copies:
        copy.wait()


VMEM = pl.BlockSpec(memory_space=pltpu.VMEM)
SMEM = pl.BlockSpec(memory_space=pltpu.SMEM)


def struct(shape, dtype=F32):
    return jax.ShapeDtypeStruct(shape, dtype)


FACES = [struct((2, 8, LANES)), struct((2, 3, LX, 128)), struct((4, 8, 128))]
FIELD = struct((NPOP, LX, LANES))
WIDE = pltpu.VMEM((NPOP, 32, LANES + 256), F32)


def call(kernel, ins, outs, scratch, **params):
    return pl.pallas_call(
        kernel, out_shape=outs, in_specs=ins,
        out_specs=jax.tree.map(lambda _: VMEM, outs), scratch_shapes=scratch,
        compiler_params=pltpu.CompilerParams(vmem_limit_bytes=56 * 2**20, **params))


def halo(faces, number):
    sem = pltpu.SemaphoreType.DMA((8,))
    return call(halo_kernel, [VMEM] * 3, FACES, [sem, sem],
                collective_id=number, has_side_effects=True)(*faces)


def per_device(held_flow, held_heat, coarse_flow, coarse_heat, pair_mask, moved_count, refine_src):
    dma = pltpu.SemaphoreType.DMA
    own, part_a, part_b = call(
        pack_kernel, [VMEM] * 4,
        [struct((2, NPOP, LX, 128), BF16), struct((8, ROWS_A, 128), BF16),
         struct((8, ROWS_B, 128), BF16)],
        [pltpu.VMEM((NPOP * 32, 128), F32)])(
            held_flow, held_heat, coarse_flow.reshape(19, 4096), coarse_heat.reshape(7, 4096))
    ns = len(SPLITS)
    arrived, picked_a, picked_b = call(
        blocks_kernel, [SMEM] * 3 + [VMEM] * 3,
        [struct((2, NPOP, LX, 128), BF16), struct((2, ROWS_A, 128), BF16),
         struct((2, ROWS_B, 128), BF16)],
        [pltpu.VMEM((2 * STEPS, NPOP, LX, 128), BF16), pltpu.VMEM((2 * STEPS, NPOP, LX, 128), BF16),
         pltpu.VMEM((4, 8, ROWS_A, 128), BF16), pltpu.VMEM((4, 8, ROWS_B, 128), BF16),
         pltpu.SMEM((13, 1, 1, 4), jnp.int32),
         pltpu.VMEM((8, 2, ROWS_A, 128), BF16), pltpu.VMEM((8, 2, ROWS_B, 128), BF16),
         pltpu.VMEM((8, 2, ROWS_A, 128), BF16), pltpu.VMEM((8, 2, ROWS_B, 128), BF16),
         dma((2 * STEPS, ns)), dma((2 * STEPS, ns)), dma((13,)), dma((13,)),
         dma((2, 4)), dma((2, 4)), dma((2, 8)), dma((2, 8))],
        collective_id=0, has_side_effects=True)(
            jnp.asarray(RING_TABLE), pair_mask, refine_src, own, part_a, part_b)
    relaxed, *faces = call(
        start_kernel, [SMEM] * 2 + [VMEM] * 5, [FIELD] + FACES,
        [pltpu.VMEM((NPOP * LX, 128), F32), pltpu.VMEM((NPOP * LX, 512), BF16),
         pltpu.VMEM((512, LANES), BF16), pltpu.VMEM((NPOP * LX, LANES), F32)])(
            refine_src, moved_count, held_flow, held_heat, arrived, picked_a, picked_b)
    faces = halo(faces, 1)
    relaxed, *faces = call(step_kernel, [VMEM] * 4, [FIELD] + FACES, [WIDE])(relaxed, *faces)
    faces = halo(faces, 2)
    return tuple(call(final_kernel, [VMEM] * 4,
                      [struct((19, LX, LANES)), struct((7, LX, LANES))], [WIDE])(relaxed, *faces))


def solution(mesh):
    return jax.shard_map(
        per_device,
        mesh=mesh,
        in_specs=(
            P(None, "brow", "bcol"),
            P(None, "brow", "bcol"),
            P(None, "brow", "bcol", None),
            P(None, "brow", "bcol", None),
            P("brow"),
            P("brow", "bcol"),
            P("brow", "bcol", None),
        ),
        out_specs=(P(None, "brow", "bcol"), P(None, "brow", "bcol")),
        check_vma=False,
    )
```

```python
import jax
import jax.numpy as jnp
import numpy as np
from jax import lax
from jax.experimental import pallas as pl
from jax.experimental.pallas import tpu as pltpu
from jax.sharding import PartitionSpec as P

MESH = pl.DeviceIdType.MESH
F32 = jnp.float32
BF16 = jnp.bfloat16

NPOP = 26
LX = 16
LANES = 1024
RING = 16
STEPS = 4
SPLITS = ((0, 9), (9, 18), (18, 26))
ROWS_A, ROWS_B = 64, 48

flow_cx = [0, 1, -1, 0, 0, 0, 0, 1, -1, 1, -1, 1, -1, 1, -1, 0, 0, 0, 0]
flow_cy = [0, 0, 0, 1, -1, 0, 0, 1, -1, -1, 1, 0, 0, 0, 0, 1, -1, 1, -1]
flow_cz = [0, 0, 0, 0, 0, 1, -1, 0, 0, 0, 0, 1, -1, -1, 1, 1, -1, -1, 1]
flow_weight = [1.0 / 3.0] + [1.0 / 18.0] * 6 + [1.0 / 36.0] * 12
flow_reverse = [0, 2, 1, 4, 3, 6, 5, 8, 7, 10, 9, 12, 11, 14, 13, 16, 15, 18, 17]
heat_reverse = [0, 2, 1, 4, 3, 6, 5]
POP_CX = flow_cx + flow_cx[:7]
POP_CY = flow_cy + flow_cy[:7]
POP_CZ = flow_cz + flow_cz[:7]
POP_REV = flow_reverse + [19 + r for r in heat_reverse]
X_UP = [i for i in range(NPOP) if POP_CX[i] == 1]
X_DOWN = [i for i in range(NPOP) if POP_CX[i] == -1]
Y_UP = [i for i in range(NPOP) if POP_CY[i] == 1]
Y_DOWN = [i for i in range(NPOP) if POP_CY[i] == -1]
CORNERS = ((7, 1, 1), (8, -1, -1), (9, 1, -1), (10, -1, 1))
tau_flow = 0.8
tau_heat = 0.7
tau_flow_coarse = 0.65
tau_heat_coarse = 0.6
buoyancy = 0.01
heat_ref = 7.0


def ring_jobs(mask):
    ways = ([], [])
    ties = []
    for c in range(RING):
        for h in range(2):
            start = c if mask % 2 == 0 else (c + 1 - 2 * h) % RING
            d = ((c ^ mask) - start) % RING
            if d == RING // 2:
                ties.append((d // 2, start, c, h))
            elif d:
                ways[d > RING // 2].append((min(d, RING - d) // 2, start, c, h))
    return ways, ties


def ring_seats(packets, sign):
    packets = sorted(packets, key=lambda p: (-p[0], sign * p[1] % RING, p[2], p[3]))
    busy = {}
    out = {}

    def place(n):
        if n == len(packets):
            return True
        jumps, start, c, h = packets[n]
        for t0 in range(STEPS - jumps + 1):
            taken = busy.setdefault((start - sign * 2 * t0) % RING, [])
            if all(t0 + jumps <= a or b <= t0 for a, b in taken):
                taken.append((t0, t0 + jumps))
                out[n] = t0
                if place(n + 1):
                    return True
                taken.pop()
        return False

    return [p + (out[n],) for n, p in enumerate(packets)] if place(0) else None


def ring_tables():
    word = np.zeros((RING, RING), np.int32)
    land = np.zeros((2, RING, RING), np.int32)
    for mask in range(1, RING):
        ways, ties = ring_jobs(mask)
        for pick in ((0, 1), (1, 0), (0, 0), (1, 1)):
            plan = [ring_seats(ways[w] + [p for p in ties if pick[p[3]] == w], 1 - 2 * w)
                    for w in range(2)]
            if None not in plan:
                break
        assert None not in plan
        for c in range(RING):
            for h in range(2):
                land[h, mask, c] = 2 * STEPS + h
        for w in range(2):
            for jumps, start, c, h, t0 in plan[w]:
                word[mask, start] |= (1 + h) << (2 * (w * STEPS + t0))
                land[h, mask, c ^ mask] = w * STEPS + t0 + jumps - 1
    return np.stack([word.reshape(-1), land[0].reshape(-1), land[1].reshape(-1)])


RING_TABLE = ring_tables()


def lane_ids(rows):
    return lax.broadcasted_iota(jnp.int32, (rows, 128), 1)


def total(values):
    values = list(values)
    while len(values) > 1:
        values = [a + b for a, b in zip(values[::2], values[1::2])] + (
            [values[-1]] if len(values) % 2 else [])
    return values[0]


def moments(f, push):
    rho = total(f[:19])
    heat = total(f[19:])

    def along(c):
        ups = [f[i] for i in range(19) if c[i] == 1]
        downs = [f[i] for i in range(19) if c[i] == -1]
        return total([u - d for u, d in zip(ups, downs)])

    mx, my, mz = along(flow_cx), along(flow_cy), along(flow_cz)
    force = None
    if push:
        force = buoyancy * rho * (heat - heat_ref)
        mz = mz + 0.5 * force
    inv = 1.0 / rho
    return rho, heat, force, (mx, my, mz), (mx * inv, my * inv, mz * inv)


def dot_dir(i, v):
    terms = []
    for c, a in zip((flow_cx[i], flow_cy[i], flow_cz[i]), v):
        if c:
            terms.append((c, a))
    out = terms[0][1] if terms[0][0] > 0 else -terms[0][1]
    for c, a in terms[1:]:
        out = out + a if c > 0 else out - a
    return out


PAIRS = [(1, 2), (3, 4), (5, 6), (7, 8), (9, 10), (11, 12), (13, 14), (15, 16), (17, 18)]


def collide(f):
    rho, heat, force, mom, vel = moments(f, True)
    rate = 1.0 / tau_flow
    keep = 1.0 - rate
    gain = 1.0 - 0.5 / tau_flow
    speed = mom[0] * vel[0] + mom[1] * vel[1] + mom[2] * vel[2]
    common = rate * rho - (1.5 * rate) * speed - (3.0 * gain) * force * vel[2]
    fgain = (9.0 * gain) * force
    fodd = (3.0 * gain) * force
    out = [None] * NPOP
    out[0] = keep * f[0] + flow_weight[0] * common
    for i, j in PAIRS:
        w = flow_weight[i]
        cu = dot_dir(i, vel)
        cm = dot_dir(i, mom)
        bracket = (4.5 * rate) * cm
        odd = (3.0 * rate) * cm
        if flow_cz[i] == 1:
            bracket = bracket + fgain
            odd = odd + fodd
        elif flow_cz[i] == -1:
            bracket = bracket - fgain
            odd = odd - fodd
        even = common + bracket * cu
        out[i] = keep * f[i] + w * (even + odd)
        out[j] = keep * f[j] + w * (even - odd)
    hrate = 1.0 / tau_heat
    hkeep = 1.0 - hrate
    out[19] = hkeep * f[19] + (0.25 * hrate) * heat
    side = (0.125 * hrate) * heat
    for k, a in zip((20, 22, 24), vel):
        tilt = 4.0 * side * a
        out[k] = hkeep * f[k] + (side + tilt)
        out[k + 1] = hkeep * f[k + 1] + (side - tilt)
    return out


def explode(f):
    rho, heat, _, mom, vel = moments(f, False)
    blend = tau_flow / (2.0 * tau_flow_coarse)
    rest = 1.0 - blend
    speed = mom[0] * vel[0] + mom[1] * vel[1] + mom[2] * vel[2]
    common = rest * rho - (1.5 * rest) * speed
    out = [None] * NPOP
    out[0] = blend * f[0] + flow_weight[0] * common
    for i, j in PAIRS:
        w = flow_weight[i]
        cu = dot_dir(i, vel)
        cm = dot_dir(i, mom)
        even = common + ((4.5 * rest) * cm) * cu
        odd = (3.0 * rest) * cm
        out[i] = blend * f[i] + w * (even + odd)
        out[j] = blend * f[j] + w * (even - odd)
    hblend = tau_heat / (2.0 * tau_heat_coarse)
    hrest = 1.0 - hblend
    out[19] = hblend * f[19] + (0.25 * hrest) * heat
    side = (0.125 * hrest) * heat
    for k, a in zip((20, 22, 24), vel):
        tilt = 4.0 * side * a
        out[k] = hblend * f[k] + (side + tilt)
        out[k + 1] = hblend * f[k + 1] + (side - tilt)
    return out


def held_tile(hf, hh, p, rows, cols):
    return hf[p, rows, cols] if p < 19 else hh[p - 19, rows, cols]


def pack_trade(hf, hh, own):
    group = lane_ids(LX) % 64 // 16
    for p in range(NPOP):
        for q in range(2):
            packed = None
            for kk in range(4):
                k = 4 * q + kk
                tile = held_tile(hf, hh, p, slice(None), slice(128 * k, 128 * k + 128))
                if kk == 0:
                    packed = tile
                else:
                    packed = jnp.where(group == kk, pltpu.roll(tile, 16 * kk, 1), packed)
            own[q, p] = packed.astype(BF16)


def pack_coarse(cf, ch, spread, put):
    for t in range(32):
        cols = slice(128 * t, 128 * t + 128)
        flow = cf[:, cols].astype(F32)
        heat = ch[:, cols].astype(F32)
        spread[pl.ds(t, 8, stride=32), :] = flow[0:8]
        spread[pl.ds(8 * 32 + t, 8, stride=32), :] = flow[8:16]
        spread[pl.ds(16 * 32 + t, 3, stride=32), :] = flow[16:19]
        spread[pl.ds(19 * 32 + t, 7, stride=32), :] = heat
    high = lane_ids(8) // 8 % 2 == 1
    zeros = jnp.zeros((8, 128), F32)
    for ox in range(2):
        for oy in range(2):
            low_rows, high_rows = [], []
            for pair in range(13):
                a = spread[pl.ds(pair * 32 + 16 * ox + oy, 8, stride=2), :]
                b = spread[pl.ds((pair + 13) * 32 + 16 * ox + oy, 8, stride=2), :]
                low_rows.append(jnp.where(high, pltpu.roll(b, 8, 1), a))
                high_rows.append(jnp.where(high, b, pltpu.roll(a, 120, 1)))
            for oz, rows in ((0, low_rows), (1, high_rows)):
                rows = rows + [zeros]
                for i in range(7):
                    put(4 * ox + 2 * oy + oz, i,
                        jnp.concatenate([rows[2 * i], rows[2 * i + 1]], axis=0).astype(BF16))


def place():
    me = lax.axis_index("brow")
    col = lax.axis_index("bcol")
    return me // 8, me // 2 % 4, me % 2, col


def row_of(x, y, k):
    return (x * 4 + y) * 2 + k


OFFSETS = [(d, dk) for d in range(4) for dk in range(2)]


OFFSETS = [(d, dk) for d in range(4) for dk in range(2)]


def edge_faces(field, xs, ys, cs, base, lead):
    low = lane_ids(LX) < 64
    for n, p in enumerate(X_UP):
        xs[0, n:n + 1, :] = field[p, base + 15:base + 16, lead:lead + LANES]
    for n, p in enumerate(X_DOWN):
        xs[1, n:n + 1, :] = field[p, base:base + 1, lead:lead + LANES]
    rows = slice(base, base + LX)
    last = slice(lead + LANES - 128, lead + LANES)
    first = slice(lead, lead + 128)
    for n in range(3):
        a, b = Y_UP[2 * n], Y_UP[2 * n + 1]
        ys[0, n] = jnp.where(low, pltpu.roll(field[a, rows, last], 64, 1), field[b, rows, last])
        a, b = Y_DOWN[2 * n], Y_DOWN[2 * n + 1]
        ys[1, n] = jnp.where(low, field[a, rows, first], pltpu.roll(field[b, rows, first], 64, 1))
    for n, (p, sx, sy) in enumerate(CORNERS):
        cs[n] = field[p, base + 8:base + 16, last] if (sx, sy) == (1, 1) else (
            field[p, base:base + 8, first] if (sx, sy) == (-1, -1) else (
                field[p, base + 8:base + 16, first] if (sx, sy) == (1, -1) else
                field[p, base:base + 8, last]))


def widen(relaxed, xr, yr, cr, wide):
    for p in range(NPOP):
        wide[p, 8:24, 128:128 + LANES] = relaxed[p]
    fill_edges(xr, yr, cr, wide)


def fill_edges(xr, yr, cr, wide):
    for n, (p, sx, sy) in enumerate(CORNERS):
        rows = slice(0, 8) if sx == 1 else slice(24, 32)
        cols = slice(0, 128) if sy == 1 else slice(128 + LANES, 256 + LANES)
        wide[p, rows, cols] = cr[n]
    for n, p in enumerate(X_UP):
        wide[p, 7:8, 128:128 + LANES] = xr[0, n:n + 1, :]
    for n, p in enumerate(X_DOWN):
        wide[p, 24:25, 128:128 + LANES] = xr[1, n:n + 1, :]
    for n in range(3):
        a, b = Y_UP[2 * n], Y_UP[2 * n + 1]
        wide[a, 8:24, 0:128] = pltpu.roll(yr[0, n], 64, 1)
        wide[b, 8:24, 0:128] = yr[0, n]
        a, b = Y_DOWN[2 * n], Y_DOWN[2 * n + 1]
        wide[a, 8:24, 128 + LANES:256 + LANES] = yr[1, n]
        wide[b, 8:24, 128 + LANES:256 + LANES] = pltpu.roll(yr[1, n], 64, 1)


def pulled(wide, p, rt, k):
    cx, cy, cz = POP_CX[p], POP_CY[p], POP_CZ[p]
    rows = slice(8 + 8 * rt - cx, 16 + 8 * rt - cx)

    def tile(e):
        return pl.ds(pl.multiple_of(128 * e, 128), 128)

    low = lane_ids(8) < 64
    value = wide[p, rows, tile(k + 1)]
    shift = 0
    if cy == 1:
        value = jnp.where(low, value, wide[p, rows, tile(k)])
        shift = 64
    elif cy == -1:
        value = jnp.where(low, wide[p, rows, tile(k + 2)], value)
        shift = 64
    shift = (shift + cz) % 128
    if shift:
        value = pltpu.roll(value, shift, 1)
    if cz:
        wall = lane_ids(8) % 64 == (0 if cz == 1 else 63)
        back = wide[POP_REV[p], 8 + 8 * rt:16 + 8 * rt, tile(k + 1)]
        value = jnp.where(wall, back, value)
    return value


def by_slot(lane, picks):
    slot = lane % 64 // 16
    return jnp.where(slot == 0, picks[0], jnp.where(
        slot == 1, picks[1], jnp.where(slot == 2, picks[2], picks[3])))


def first_and_last(values):
    first, last = values[3], values[0]
    for j in (2, 1, 0):
        first = jnp.where(values[j] >= 0, values[j], first)
    for j in (1, 2, 3):
        last = jnp.where(values[j] >= 0, values[j], last)
    return first, last


def one_hots(children, trades, child, trade):
    for t in range(8):
        lane = lax.broadcasted_iota(jnp.int32, (1, 128), 1)
        yy = 2 * t + lane // 64
        want = yy // 2 * 16 + lane % 16 // 2 + by_slot(lane, child)
        row = lax.broadcasted_iota(jnp.int32, (128, 128), 0)
        hot = jnp.where(row == want, 1.0, 0.0).astype(BF16)
        cols = slice(128 * t, 128 * t + 128)
        children[0:128, cols] = hot
        children[128:256, cols] = hot
        row = lax.broadcasted_iota(jnp.int32, (256, 128), 0)
        z = lane % 64
        want = yy // 8 * 128 + yy % 2 * 64 + yy % 8 // 2 * 16 + z
        want = jnp.where(z < 16, want + trade, 1 << 20)
        trades[:, cols] = jnp.where(row == want, 1.0, 0.0).astype(BF16)


def refine(picked_a, picked_b, spread, left):
    high = lane_ids(8) // 8 % 2 == 1
    values = [None] * NPOP
    for pair in range(13):
        part, row = (picked_a, 8 * pair) if pair < 8 else (picked_b, 8 * pair - 64)
        base = row // 16 * 16
        a = part[0, base:base + 16, :].astype(F32)[row - base:row - base + 8]
        b = part[1, base:base + 16, :].astype(F32)[row - base:row - base + 8]
        values[pair] = jnp.where(high, pltpu.roll(b, 8, 1), a)
        values[pair + 13] = jnp.where(high, b, pltpu.roll(a, 120, 1))
    for p, value in enumerate(explode(values)):
        spread[pl.ds(16 * p, 8, stride=2), :] = value
        spread[pl.ds(16 * p + 1, 8, stride=2), :] = value
    for p in range(NPOP):
        rows = slice(16 * p, 16 * p + 16)
        value = spread[rows, :]
        top = value.astype(BF16)
        left[rows, 0:128] = top
        left[rows, 128:256] = (value - top.astype(F32)).astype(BF16)


def main_kernel(table, mask_ref, moved, codes_in, hf, hh, cf, ch,
                relaxed, xr2, yr2, cr2,
                own, landing, leaving, ready, held_a, held_b, codes,
                stage_a, stage_b, got_a, got_b, picked_a, picked_b,
                spread, left, children, trades, fresh, wide,
                xs1, ys1, cs1, xr1, yr1, cr1, xs2, ys2, cs2,
                ring_send, ring_recv, code_send, code_recv, one_send, one_recv,
                two_send, two_recv, halo_send, halo_recv):
    x, y, k, col = place()
    me = row_of(x, y, k)
    x_group = [row_of(x, (y + d) % 4, (k + dk) % 2) for d, dk in OFFSETS]
    y_group = [row_of((x + d) % 4, y, (k + dk) % 2) for d, dk in OFFSETS]
    peers = x_group[1:] + y_group[2:]
    near_row = {1: (me + 1) % 32, -1: (me + 31) % 32, 0: me}
    near_col = {d: (col + d + RING) % RING for d in (-2, -1, 0, 1, 2)}

    barrier = pltpu.get_barrier_semaphore()
    greeted = [(me, near_col[d]) for d in (-2, -1, 1, 2)] + [(peer, col) for peer in peers]
    greeted += [(near_row[sx], near_col[sy]) for sx in (-1, 1) for sy in (-1, 0, 1)]
    for device in greeted:
        pl.semaphore_signal(barrier, inc=1, device_id=device, device_id_type=MESH)

    pending = []

    def send(source, target, sends, recvs, device):
        copy = pltpu.make_async_remote_copy(
            src_ref=source, dst_ref=target, send_sem=sends, recv_sem=recvs,
            device_id=device, device_id_type=MESH)
        copy.start()
        pending.append(copy)
        return copy

    entry = mask_ref[0] * RING + col
    word = table[0, entry]
    odd = mask_ref[0] & 1
    ring = {}

    def ring_send_slot(source, slot, s, device):
        lo, hi = SPLITS[s]
        ring[slot, s] = send(source.at[lo:hi], landing.at[slot, lo:hi],
                             ring_send.at[slot, s], ring_recv.at[slot, s], device)

    def ring_step(step):
        for s, (lo, hi) in enumerate(SPLITS):
            if step == 0:
                for h in range(2):
                    ring[2 * STEPS + h, s].wait_recv()
                    ready[h, lo:hi] = jnp.where(odd == 1, landing[2 * STEPS + h, lo:hi],
                                                own[h, lo:hi])
            for way in range(2):
                slot = way * STEPS + step
                code = (word >> (2 * slot)) & 3
                other = ready[0, lo:hi]
                if step:
                    ring[slot - 1, s].wait_recv()
                    other = jnp.where(code == 1, other, landing[slot - 1, lo:hi])
                leaving[slot, lo:hi] = jnp.where(code == 2, ready[1, lo:hi], other)
                ring_send_slot(leaving.at[slot], slot, s, (me, near_col[2 - 4 * way]))

    pack_trade(hf, hh, own)
    pl.semaphore_wait(barrier, len(greeted))
    for s in range(len(SPLITS)):
        for h in range(2):
            ring_send_slot(own.at[h], 2 * STEPS + h, s, (me, near_col[1 - 2 * h]))
    code_copies = [send(codes_in, codes.at[n], code_send.at[n], code_recv.at[n], (peer, col))
                   for n, peer in enumerate(peers)]

    def put(octant, i, value):
        if i < 4:
            held_a[0, octant, 16 * i:16 * i + 16, :] = value
        else:
            held_b[0, octant, 16 * (i - 4):16 * (i - 4) + 16, :] = value

    pack_coarse(cf, ch, spread, put)
    one_copies = []
    for d in (2, 1, 3):
        one_copies.append(send(held_a.at[0], held_a.at[d], one_send.at[0, d], one_recv.at[0, d],
                               (row_of((x + d) % 4, y, k), col)))
        one_copies.append(send(held_b.at[0], held_b.at[d], one_send.at[1, d], one_recv.at[1, d],
                               (row_of(x, (y + d) % 4, k), col)))
    ring_step(0)

    source = [codes_in[0, 0, j] for j in range(4)]
    refined = [jnp.where(v >= 0, 1, 0) for v in source]
    rank = [0]
    for j in range(3):
        rank.append(rank[-1] + refined[j])
    child = [jnp.where(refined[j] == 1, rank[j] * 8, 1 << 20) for j in range(4)]
    trade = jnp.where((moved[0, 0] > 0) & (refined[0] == 0), 0, 1 << 20)
    one_hots(children, trades, child, trade)
    ring_step(1)

    for copy in code_copies + one_copies:
        copy.wait_recv()
    mine = first_and_last(source)
    two_copies = []
    for n, (d, dk) in enumerate(OFFSETS):
        for part, (group, stage, got, held, home) in enumerate((
                (x_group, stage_a, got_a, held_a, x), (y_group, stage_b, got_b, held_b, y))):
            if n == 0:
                pair = mine
            else:
                back = OFFSETS.index(((4 - d) % 4, dk))
                row = back - 1 if part == 0 or d == 0 else 7 + back - 2
                pair = first_and_last([codes[row, 0, 0, j] for j in range(4)])
            for s, code in enumerate(pair):
                parent = (code >> 6) & 3 if part == 0 else (code >> 4) & 3
                value = held[(home - parent + 4) & 3, code & 7]
                if n == 0:
                    got[0, s] = value
                else:
                    stage[n, s] = value
            if n:
                two_copies.append(send(stage.at[n], got.at[n], two_send.at[part, n],
                                       two_recv.at[part, n], (group[n], col)))
    ring_step(2)
    ring_step(3)

    for copy in two_copies:
        copy.wait_recv()
    for s, code in enumerate(mine):
        core = ((code >> 3) & 1) ^ k
        picked_a[s] = got_a[((y - ((code >> 4) & 3) + 4) & 3) * 2 + core, s]
        picked_b[s] = got_b[((x - ((code >> 6) & 3) + 4) & 3) * 2 + core, s]
    refine(picked_a, picked_b, spread, left)
    for t in range(4):
        cols = slice(256 * t, 256 * t + 256)
        fresh[:, cols] = jnp.dot(left[...], children[:, cols], preferred_element_type=F32)
    keep = [1 - refined[j] for j in range(4)]
    keep[0] = jnp.where(moved[0, 0] > 0, 0, keep[0])
    kept = by_slot(lane_ids(8), keep) == 1

    def merge(t, carry):
        cols = pl.ds(pl.multiple_of(128 * t, 128), 128)
        for p in range(NPOP):
            for rt in range(2):
                rows = slice(16 * p + 8 * rt, 16 * p + 8 * rt + 8)
                fresh[rows, cols] = jnp.where(
                    kept, held_tile(hf, hh, p, slice(8 * rt, 8 * rt + 8), cols),
                    fresh[rows, cols])
        return carry

    lax.fori_loop(0, 8, merge, 0)

    for way in range(2):
        for s in range(len(SPLITS)):
            ring[way * STEPS + STEPS - 1, s].wait_recv()
    for h in range(2):
        left[:, 128 * h:128 * h + 128] = landing[table[1 + h, entry]].reshape(NPOP * LX, 128)
    for t in range(4):
        cols = slice(256 * t, 256 * t + 256)
        fresh[:, cols] += jnp.dot(left[...], trades[:, cols], preferred_element_type=F32)

    def exchange(turn, faces, arrivals):
        (xs, ys, cs), (xr, yr, cr) = faces, arrivals
        moves = [(cs.at[n], cr.at[n], sx, sy) for n, (p, sx, sy) in enumerate(CORNERS)]
        moves += [(xs.at[0], xr.at[0], 1, 0), (xs.at[1], xr.at[1], -1, 0),
                  (ys.at[0], yr.at[0], 0, 1), (ys.at[1], yr.at[1], 0, -1)]
        return [send(a, b, halo_send.at[turn, n], halo_recv.at[turn, n],
                     (near_row[sx], near_col[sy])) for n, (a, b, sx, sy) in enumerate(moves)]

    def first_step(t, carry):
        cols = pl.ds(pl.multiple_of(128 * t, 128), 128)
        wide_cols = pl.ds(pl.multiple_of(128 * t + 128, 128), 128)
        for rt in range(2):
            f = [fresh[16 * p + 8 * rt:16 * p + 8 * rt + 8, cols] for p in range(NPOP)]
            for p, value in enumerate(collide(f)):
                wide[p, 8 + 8 * rt:16 + 8 * rt, wide_cols] = value
        return carry

    lax.fori_loop(0, 8, first_step, 0)
    edge_faces(wide, xs1, ys1, cs1, 8, 128)
    for copy in exchange(0, (xs1, ys1, cs1), (xr1, yr1, cr1)):
        copy.wait_recv()
    fill_edges(xr1, yr1, cr1, wide)

    def second_step(t, carry):
        cols = pl.ds(pl.multiple_of(128 * t, 128), 128)
        for rt in range(2):
            f = [pulled(wide, p, rt, t) for p in range(NPOP)]
            for p, value in enumerate(collide(f)):
                relaxed[p, 8 * rt:8 * rt + 8, cols] = value
        return carry

    lax.fori_loop(0, 8, second_step, 0)
    edge_faces(relaxed, xs2, ys2, cs2, 0, 0)
    for copy in exchange(1, (xs2, ys2, cs2), (xr2, yr2, cr2)):
        copy.wait_recv()
    for copy in pending:
        copy.wait_send()


def final_kernel(relaxed_in, xr, yr, cr, out_flow, out_heat, wide):
    widen(relaxed_in, xr, yr, cr, wide)

    def body(k, carry):
        cols = pl.ds(pl.multiple_of(128 * k, 128), 128)
        for rt in range(2):
            for p in range(NPOP):
                value = pulled(wide, p, rt, k)
                if p < 19:
                    out_flow[p, 8 * rt:8 * rt + 8, cols] = value
                else:
                    out_heat[p - 19, 8 * rt:8 * rt + 8, cols] = value
        return carry

    lax.fori_loop(0, 8, body, 0)


VMEM = pl.BlockSpec(memory_space=pltpu.VMEM)
SMEM = pl.BlockSpec(memory_space=pltpu.SMEM)


def struct(shape, dtype=F32):
    return jax.ShapeDtypeStruct(shape, dtype)


FACES = [struct((2, 8, LANES)), struct((2, 3, LX, 128)), struct((4, 8, 128))]
FIELD = struct((NPOP, LX, LANES))
WIDE = pltpu.VMEM((NPOP, 32, LANES + 256), F32)


def call(kernel, ins, outs, scratch, **params):
    return pl.pallas_call(
        kernel, out_shape=outs, in_specs=ins,
        out_specs=jax.tree.map(lambda _: VMEM, outs), scratch_shapes=scratch,
        compiler_params=pltpu.CompilerParams(vmem_limit_bytes=56 * 2**20, **params))


def vmem(spec):
    return pltpu.VMEM(spec.shape, spec.dtype)


def per_device(held_flow, held_heat, coarse_flow, coarse_heat, pair_mask, moved_count, refine_src):
    dma = pltpu.SemaphoreType.DMA
    ns = len(SPLITS)
    slots = 2 * STEPS + 2
    block = (NPOP, LX, 128)
    relaxed, *faces = call(
        main_kernel, [SMEM] * 4 + [VMEM] * 4, [FIELD] + FACES,
        [pltpu.VMEM((2,) + block, BF16), pltpu.VMEM((slots,) + block, BF16),
         pltpu.VMEM((2 * STEPS,) + block, BF16), pltpu.VMEM((2,) + block, BF16),
         pltpu.VMEM((4, 8, ROWS_A, 128), BF16), pltpu.VMEM((4, 8, ROWS_B, 128), BF16),
         pltpu.SMEM((13, 1, 1, 4), jnp.int32),
         pltpu.VMEM((8, 2, ROWS_A, 128), BF16), pltpu.VMEM((8, 2, ROWS_B, 128), BF16),
         pltpu.VMEM((8, 2, ROWS_A, 128), BF16), pltpu.VMEM((8, 2, ROWS_B, 128), BF16),
         pltpu.VMEM((2, ROWS_A, 128), BF16), pltpu.VMEM((2, ROWS_B, 128), BF16),
         pltpu.VMEM((NPOP * 32, 128), F32), pltpu.VMEM((NPOP * LX, 256), BF16),
         pltpu.VMEM((256, LANES), BF16), pltpu.VMEM((256, LANES), BF16),
         pltpu.VMEM((NPOP * LX, LANES), F32), WIDE]
        + [vmem(f) for f in FACES * 3]
        + [dma((slots, ns)), dma((slots, ns)), dma((13,)), dma((13,)),
           dma((2, 4)), dma((2, 4)), dma((2, 8)), dma((2, 8)), dma((2, 8)), dma((2, 8))],
        collective_id=0, has_side_effects=True)(
            jnp.asarray(RING_TABLE), pair_mask, moved_count, refine_src,
            held_flow, held_heat, coarse_flow.reshape(19, 4096), coarse_heat.reshape(7, 4096))
    return tuple(call(final_kernel, [VMEM] * 4,
                      [struct((19, LX, LANES)), struct((7, LX, LANES))], [WIDE])(relaxed, *faces))


def solution(mesh):
    return jax.shard_map(
        per_device,
        mesh=mesh,
        in_specs=(
            P(None, "brow", "bcol"),
            P(None, "brow", "bcol"),
            P(None, "brow", "bcol", None),
            P(None, "brow", "bcol", None),
            P("brow"),
            P("brow", "bcol"),
            P("brow", "bcol", None),
        ),
        out_specs=(P(None, "brow", "bcol"), P(None, "brow", "bcol")),
        check_vma=False,
    )
```

```python
import jax
import jax.numpy as jnp
import numpy as np
from jax import lax
from jax.experimental import pallas as pl
from jax.experimental.pallas import tpu as pltpu
from jax.sharding import PartitionSpec as P

MESH = pl.DeviceIdType.MESH
F32 = jnp.float32
BF16 = jnp.bfloat16

NPOP = 26
LX = 16
LANES = 1024
RING = 16
JUMPS = (1, 2, 2, 2, 1)
STEPS = len(JUMPS)
SPLITS = ((0, 9), (9, 18), (18, 26))
ROWS_A, ROWS_B = 64, 48

flow_cx = [0, 1, -1, 0, 0, 0, 0, 1, -1, 1, -1, 1, -1, 1, -1, 0, 0, 0, 0]
flow_cy = [0, 0, 0, 1, -1, 0, 0, 1, -1, -1, 1, 0, 0, 0, 0, 1, -1, 1, -1]
flow_cz = [0, 0, 0, 0, 0, 1, -1, 0, 0, 0, 0, 1, -1, -1, 1, 1, -1, -1, 1]
flow_weight = [1.0 / 3.0] + [1.0 / 18.0] * 6 + [1.0 / 36.0] * 12
flow_reverse = [0, 2, 1, 4, 3, 6, 5, 8, 7, 10, 9, 12, 11, 14, 13, 16, 15, 18, 17]
heat_reverse = [0, 2, 1, 4, 3, 6, 5]
POP_CX = flow_cx + flow_cx[:7]
POP_CY = flow_cy + flow_cy[:7]
POP_CZ = flow_cz + flow_cz[:7]
POP_REV = flow_reverse + [19 + r for r in heat_reverse]
X_UP = [i for i in range(NPOP) if POP_CX[i] == 1]
X_DOWN = [i for i in range(NPOP) if POP_CX[i] == -1]
Y_UP = [i for i in range(NPOP) if POP_CY[i] == 1]
Y_DOWN = [i for i in range(NPOP) if POP_CY[i] == -1]
CORNERS = ((7, 1, 1), (8, -1, -1), (9, 1, -1), (10, -1, 1))
tau_flow = 0.8
tau_heat = 0.7
tau_flow_coarse = 0.65
tau_heat_coarse = 0.6
buoyancy = 0.01
heat_ref = 7.0


def ring_plan(mask):
    travels = {d: [] for d in range(RING // 2 + 1)}
    for picks in range(1 << STEPS):
        steps = tuple(t for t in range(STEPS) if picks >> t & 1)
        travels.setdefault(sum(JUMPS[t] for t in steps), []).append(steps)
    for d in travels:
        travels[d].sort(key=lambda steps: (len(steps), steps))
    packets = []
    for c in range(RING):
        d = ((c ^ mask) - c) % RING
        for h in range(2):
            way = h if 2 * d == RING else int(2 * d > RING)
            packets.append((c, h, way, travels[min(d, RING - d)]))
    used = set()
    plan = {}

    def copies(c, way, steps):
        out = []
        for t in steps:
            out.append((way, t, c))
            c = (c + (1 - 2 * way) * JUMPS[t]) % RING
        return out

    def place(left):
        if not left:
            return True
        fits = [[steps for steps in p[3] if used.isdisjoint(copies(p[0], p[2], steps))]
                for p in left]
        n = min(range(len(left)), key=lambda i: len(fits[i]))
        c, h, way, _ = left[n]
        for steps in fits[n]:
            taken = copies(c, way, steps)
            used.update(taken)
            plan[c, h] = (way, steps, taken)
            if place(left[:n] + left[n + 1:]):
                return True
            used.difference_update(taken)
        return False

    assert place(packets)
    return plan


def ring_tables():
    code = np.zeros((RING, RING, 2 * STEPS), np.int32)
    land = np.zeros((2, RING, RING), np.int32)
    for mask in range(1, RING):
        for (c, h), (way, steps, taken) in ring_plan(mask).items():
            source = h
            for _, t, node in taken:
                code[mask, node, way * STEPS + t] = source
                source = 2 + t
            land[h, mask, c ^ mask] = way * STEPS + steps[-1]
    word = sum(code[:, :, n] << (3 * n) for n in range(2 * STEPS))
    kinds = [sorted(set(code[:, :, n].reshape(-1).tolist())) for n in range(2 * STEPS)]
    return np.stack([word.reshape(-1), land[0].reshape(-1), land[1].reshape(-1)]), kinds


RING_TABLE, RING_KINDS = ring_tables()


def lane_ids(rows):
    return lax.broadcasted_iota(jnp.int32, (rows, 128), 1)


def total(values):
    values = list(values)
    while len(values) > 1:
        values = [a + b for a, b in zip(values[::2], values[1::2])] + (
            [values[-1]] if len(values) % 2 else [])
    return values[0]


def moments(f, push):
    rho = total(f[:19])
    heat = total(f[19:])

    def along(c):
        ups = [f[i] for i in range(19) if c[i] == 1]
        downs = [f[i] for i in range(19) if c[i] == -1]
        return total([u - d for u, d in zip(ups, downs)])

    mx, my, mz = along(flow_cx), along(flow_cy), along(flow_cz)
    force = None
    if push:
        force = buoyancy * rho * (heat - heat_ref)
        mz = mz + 0.5 * force
    inv = 1.0 / rho
    return rho, heat, force, (mx, my, mz), (mx * inv, my * inv, mz * inv)


def dot_dir(i, v):
    terms = []
    for c, a in zip((flow_cx[i], flow_cy[i], flow_cz[i]), v):
        if c:
            terms.append((c, a))
    out = terms[0][1] if terms[0][0] > 0 else -terms[0][1]
    for c, a in terms[1:]:
        out = out + a if c > 0 else out - a
    return out


PAIRS = [(1, 2), (3, 4), (5, 6), (7, 8), (9, 10), (11, 12), (13, 14), (15, 16), (17, 18)]


def collide(f):
    rho, heat, force, mom, vel = moments(f, True)
    rate = 1.0 / tau_flow
    keep = 1.0 - rate
    gain = 1.0 - 0.5 / tau_flow
    speed = mom[0] * vel[0] + mom[1] * vel[1] + mom[2] * vel[2]
    common = rate * rho - (1.5 * rate) * speed - (3.0 * gain) * force * vel[2]
    fgain = (9.0 * gain) * force
    fodd = (3.0 * gain) * force
    out = [None] * NPOP
    out[0] = keep * f[0] + flow_weight[0] * common
    for i, j in PAIRS:
        w = flow_weight[i]
        cu = dot_dir(i, vel)
        cm = dot_dir(i, mom)
        bracket = (4.5 * rate) * cm
        odd = (3.0 * rate) * cm
        if flow_cz[i] == 1:
            bracket = bracket + fgain
            odd = odd + fodd
        elif flow_cz[i] == -1:
            bracket = bracket - fgain
            odd = odd - fodd
        even = common + bracket * cu
        out[i] = keep * f[i] + w * (even + odd)
        out[j] = keep * f[j] + w * (even - odd)
    hrate = 1.0 / tau_heat
    hkeep = 1.0 - hrate
    out[19] = hkeep * f[19] + (0.25 * hrate) * heat
    side = (0.125 * hrate) * heat
    for k, a in zip((20, 22, 24), vel):
        tilt = 4.0 * side * a
        out[k] = hkeep * f[k] + (side + tilt)
        out[k + 1] = hkeep * f[k + 1] + (side - tilt)
    return out


def explode(f):
    rho, heat, _, mom, vel = moments(f, False)
    blend = tau_flow / (2.0 * tau_flow_coarse)
    rest = 1.0 - blend
    speed = mom[0] * vel[0] + mom[1] * vel[1] + mom[2] * vel[2]
    common = rest * rho - (1.5 * rest) * speed
    out = [None] * NPOP
    out[0] = blend * f[0] + flow_weight[0] * common
    for i, j in PAIRS:
        w = flow_weight[i]
        cu = dot_dir(i, vel)
        cm = dot_dir(i, mom)
        even = common + ((4.5 * rest) * cm) * cu
        odd = (3.0 * rest) * cm
        out[i] = blend * f[i] + w * (even + odd)
        out[j] = blend * f[j] + w * (even - odd)
    hblend = tau_heat / (2.0 * tau_heat_coarse)
    hrest = 1.0 - hblend
    out[19] = hblend * f[19] + (0.25 * hrest) * heat
    side = (0.125 * hrest) * heat
    for k, a in zip((20, 22, 24), vel):
        tilt = 4.0 * side * a
        out[k] = hblend * f[k] + (side + tilt)
        out[k + 1] = hblend * f[k + 1] + (side - tilt)
    return out


def pack_trade(held, own, lo, hi):
    group = lane_ids(LX) % 64 // 16
    for p in range(lo, hi):
        for q in range(2):
            packed = held[p, :, 512 * q:512 * q + 128]
            for kk in range(1, 4):
                k = 4 * q + kk
                tile = held[p, :, 128 * k:128 * k + 128]
                packed = jnp.where(group == kk, pltpu.roll(tile, 16 * kk, 1), packed)
            own[q, p] = packed.astype(BF16)


def pack_coarse(cf, ch, spread, put):
    for t in range(32):
        cols = slice(128 * t, 128 * t + 128)
        flow = cf[:, cols].astype(F32)
        heat = ch[:, cols].astype(F32)
        spread[pl.ds(t, 8, stride=32), :] = flow[0:8]
        spread[pl.ds(8 * 32 + t, 8, stride=32), :] = flow[8:16]
        spread[pl.ds(16 * 32 + t, 3, stride=32), :] = flow[16:19]
        spread[pl.ds(19 * 32 + t, 7, stride=32), :] = heat
    high = lane_ids(8) // 8 % 2 == 1
    zeros = jnp.zeros((8, 128), F32)
    for ox in range(2):
        for oy in range(2):
            low_rows, high_rows = [], []
            for pair in range(13):
                a = spread[pl.ds(pair * 32 + 16 * ox + oy, 8, stride=2), :]
                b = spread[pl.ds((pair + 13) * 32 + 16 * ox + oy, 8, stride=2), :]
                low_rows.append(jnp.where(high, pltpu.roll(b, 8, 1), a))
                high_rows.append(jnp.where(high, b, pltpu.roll(a, 120, 1)))
            for oz, rows in ((0, low_rows), (1, high_rows)):
                rows = rows + [zeros]
                for i in range(7):
                    put(4 * ox + 2 * oy + oz, i,
                        jnp.concatenate([rows[2 * i], rows[2 * i + 1]], axis=0).astype(BF16))


def place():
    me = lax.axis_index("brow")
    col = lax.axis_index("bcol")
    return me // 8, me // 2 % 4, me % 2, col


def row_of(x, y, k):
    return (x * 4 + y) * 2 + k


OFFSETS = [(d, dk) for d in range(4) for dk in range(2)]


OFFSETS = [(d, dk) for d in range(4) for dk in range(2)]


def x_faces(field, xs, base, lead):
    for n, p in enumerate(X_UP):
        xs[0, n:n + 1, :] = field[p, base + 15:base + 16, lead:lead + LANES]
    for n, p in enumerate(X_DOWN):
        xs[1, n:n + 1, :] = field[p, base:base + 1, lead:lead + LANES]


def y_faces(field, ys, cs, base, lead):
    low = lane_ids(LX) < 64
    rows = slice(base, base + LX)
    last = slice(lead + LANES - 128, lead + LANES)
    first = slice(lead, lead + 128)
    for n, (p, sx, sy) in enumerate(CORNERS):
        top = base + 8 if sx == 1 else base
        cs[n] = field[p, top:top + 8, last if sy == 1 else first]
    for n in range(3):
        a, b = Y_UP[2 * n], Y_UP[2 * n + 1]
        ys[0, n] = jnp.where(low, pltpu.roll(field[a, rows, last], 64, 1), field[b, rows, last])
        a, b = Y_DOWN[2 * n], Y_DOWN[2 * n + 1]
        ys[1, n] = jnp.where(low, field[a, rows, first], pltpu.roll(field[b, rows, first], 64, 1))


def fill_edges(xr, yr, cr, wide):
    for n, (p, sx, sy) in enumerate(CORNERS):
        rows = slice(0, 8) if sx == 1 else slice(24, 32)
        cols = slice(0, 128) if sy == 1 else slice(128 + LANES, 256 + LANES)
        wide[p, rows, cols] = cr[n]
    for n, p in enumerate(X_UP):
        wide[p, 7:8, 128:128 + LANES] = xr[0, n:n + 1, :]
    for n, p in enumerate(X_DOWN):
        wide[p, 24:25, 128:128 + LANES] = xr[1, n:n + 1, :]
    for n in range(3):
        a, b = Y_UP[2 * n], Y_UP[2 * n + 1]
        wide[a, 8:24, 0:128] = pltpu.roll(yr[0, n], 64, 1)
        wide[b, 8:24, 0:128] = yr[0, n]
        a, b = Y_DOWN[2 * n], Y_DOWN[2 * n + 1]
        wide[a, 8:24, 128 + LANES:256 + LANES] = yr[1, n]
        wide[b, 8:24, 128 + LANES:256 + LANES] = pltpu.roll(yr[1, n], 64, 1)


def pulled(wide, p, rt, k):
    cx, cy, cz = POP_CX[p], POP_CY[p], POP_CZ[p]
    rows = slice(8 + 8 * rt - cx, 16 + 8 * rt - cx)

    def tile(e):
        if isinstance(e, int):
            return slice(128 * e, 128 * e + 128)
        return pl.ds(pl.multiple_of(128 * e, 128), 128)

    low = lane_ids(8) < 64
    value = wide[p, rows, tile(k + 1)]
    shift = 0
    if cy == 1:
        value = jnp.where(low, value, wide[p, rows, tile(k)])
        shift = 64
    elif cy == -1:
        value = jnp.where(low, wide[p, rows, tile(k + 2)], value)
        shift = 64
    shift = (shift + cz) % 128
    if shift:
        value = pltpu.roll(value, shift, 1)
    if cz:
        wall = lane_ids(8) % 64 == (0 if cz == 1 else 63)
        back = wide[POP_REV[p], 8 + 8 * rt:16 + 8 * rt, tile(k + 1)]
        value = jnp.where(wall, back, value)
    return value


def by_slot(lane, picks):
    slot = lane % 64 // 16
    return jnp.where(slot == 0, picks[0], jnp.where(
        slot == 1, picks[1], jnp.where(slot == 2, picks[2], picks[3])))


def first_and_last(values):
    first, last = values[3], values[0]
    for j in (2, 1, 0):
        first = jnp.where(values[j] >= 0, values[j], first)
    for j in (1, 2, 3):
        last = jnp.where(values[j] >= 0, values[j], last)
    return first, last


def one_hots(children, trades, child, trade):
    for t in range(8):
        lane = lax.broadcasted_iota(jnp.int32, (1, 128), 1)
        yy = 2 * t + lane // 64
        want = yy // 2 * 16 + lane % 16 // 2 + by_slot(lane, child)
        row = lax.broadcasted_iota(jnp.int32, (128, 128), 0)
        hot = jnp.where(row == want, 1.0, 0.0).astype(BF16)
        cols = slice(128 * t, 128 * t + 128)
        children[0:128, cols] = hot
        children[128:256, cols] = hot
        row = lax.broadcasted_iota(jnp.int32, (256, 128), 0)
        z = lane % 64
        want = yy // 8 * 128 + yy % 2 * 64 + yy % 8 // 2 * 16 + z
        want = jnp.where(z < 16, want + trade, 1 << 20)
        trades[:, cols] = jnp.where(row == want, 1.0, 0.0).astype(BF16)


def refine(picked_a, picked_b, spread, left):
    high = lane_ids(8) // 8 % 2 == 1
    values = [None] * NPOP
    for pair in range(13):
        part, row = (picked_a, 8 * pair) if pair < 8 else (picked_b, 8 * pair - 64)
        base = row // 16 * 16
        a = part[0, base:base + 16, :].astype(F32)[row - base:row - base + 8]
        b = part[1, base:base + 16, :].astype(F32)[row - base:row - base + 8]
        values[pair] = jnp.where(high, pltpu.roll(b, 8, 1), a)
        values[pair + 13] = jnp.where(high, b, pltpu.roll(a, 120, 1))
    for p, value in enumerate(explode(values)):
        spread[pl.ds(16 * p, 8, stride=2), :] = value
        spread[pl.ds(16 * p + 1, 8, stride=2), :] = value
    for p in range(NPOP):
        rows = slice(16 * p, 16 * p + 16)
        value = spread[rows, :]
        top = value.astype(BF16)
        left[rows, 0:128] = top
        left[rows, 128:256] = (value - top.astype(F32)).astype(BF16)


def main_kernel(table, mask_ref, moved, codes_in, hf, hh, cf, ch,
                relaxed_out, xr2, yr2, cr2,
                held, cfv, chv, relaxed, own, landing, leaving, held_a, held_b, codes,
                stage_a, stage_b, got_a, got_b, picked_a, picked_b,
                spread, left, children, trades, fresh, wide,
                xs1, ys1, cs1, xr1, yr1, cr1, xs2, ys2, cs2,
                ring_send, ring_recv, code_send, code_recv, one_send, one_recv,
                two_send, two_recv, halo_send, halo_recv, local):
    x, y, k, col = place()
    loads = [[pltpu.make_async_copy(hf.at[0:9], held.at[0:9], local.at[0])],
             [pltpu.make_async_copy(hf.at[9:18], held.at[9:18], local.at[1])],
             [pltpu.make_async_copy(hf.at[18:19], held.at[18:19], local.at[2]),
              pltpu.make_async_copy(hh, held.at[19:26], local.at[3])],
             [pltpu.make_async_copy(cf, cfv, local.at[4]),
              pltpu.make_async_copy(ch, chv, local.at[5])]]
    for group in loads:
        for copy in group:
            copy.start()
    me = row_of(x, y, k)
    x_group = [row_of(x, (y + d) % 4, (k + dk) % 2) for d, dk in OFFSETS]
    y_group = [row_of((x + d) % 4, y, (k + dk) % 2) for d, dk in OFFSETS]
    peers = x_group[1:] + y_group[2:]
    near_row = {1: (me + 1) % 32, -1: (me + 31) % 32, 0: me}
    near_col = {d: (col + d + RING) % RING for d in (-2, -1, 0, 1, 2)}

    barrier = pltpu.get_barrier_semaphore()
    greeted = [(me, near_col[d]) for d in (-2, -1, 1, 2)] + [(peer, col) for peer in peers]
    greeted += [(near_row[sx], near_col[sy]) for sx in (-1, 1) for sy in (-1, 0, 1)]
    for device in greeted:
        pl.semaphore_signal(barrier, inc=1, device_id=device, device_id_type=MESH)

    pending = []

    def send(source, target, sends, recvs, device):
        copy = pltpu.make_async_remote_copy(
            src_ref=source, dst_ref=target, send_sem=sends, recv_sem=recvs,
            device_id=device, device_id_type=MESH)
        copy.start()
        pending.append(copy)
        return copy

    entry = mask_ref[0] * RING + col
    word = table[0, entry]
    ring = {}

    def ring_send_of(step, s):
        lo, hi = SPLITS[s]
        for way in range(2):
            slot = way * STEPS + step
            code = (word >> (3 * slot)) & 7
            if step:
                ring[slot - 1, s].wait_recv()
            value = own[0, lo:hi]
            for kind in RING_KINDS[slot]:
                if kind == 1:
                    value = jnp.where(code == 1, own[1, lo:hi], value)
                elif kind:
                    value = jnp.where(code == kind, landing[way * STEPS + kind - 2, lo:hi], value)
            leaving[slot, lo:hi] = value
            ring[slot, s] = send(leaving.at[slot, lo:hi], landing.at[slot, lo:hi],
                                 ring_send.at[slot, s], ring_recv.at[slot, s],
                                 (me, near_col[(1 - 2 * way) * JUMPS[step]]))

    def ring_step(step):
        for s in range(len(SPLITS)):
            ring_send_of(step, s)

    for s, (lo, hi) in enumerate(SPLITS):
        for copy in loads[s]:
            copy.wait()
        pack_trade(held, own, lo, hi)
        if s == 0:
            pl.semaphore_wait(barrier, len(greeted))
        ring_send_of(0, s)
    code_copies = [send(codes_in, codes.at[n], code_send.at[n], code_recv.at[n], (peer, col))
                   for n, peer in enumerate(peers)]

    def put(octant, i, value):
        if i < 4:
            held_a[0, octant, 16 * i:16 * i + 16, :] = value
        else:
            held_b[0, octant, 16 * (i - 4):16 * (i - 4) + 16, :] = value

    for copy in loads[3]:
        copy.wait()
    pack_coarse(cfv, chv, spread, put)
    one_copies = []
    for d in (2, 1, 3):
        one_copies.append(send(held_a.at[0], held_a.at[d], one_send.at[0, d], one_recv.at[0, d],
                               (row_of((x + d) % 4, y, k), col)))
        one_copies.append(send(held_b.at[0], held_b.at[d], one_send.at[1, d], one_recv.at[1, d],
                               (row_of(x, (y + d) % 4, k), col)))
    ring_step(1)

    source = [codes_in[0, 0, j] for j in range(4)]
    refined = [jnp.where(v >= 0, 1, 0) for v in source]
    rank = [0]
    for j in range(3):
        rank.append(rank[-1] + refined[j])
    child = [jnp.where(refined[j] == 1, rank[j] * 8, 1 << 20) for j in range(4)]
    trade = jnp.where((moved[0, 0] > 0) & (refined[0] == 0), 0, 1 << 20)
    one_hots(children, trades, child, trade)
    ring_step(2)

    for copy in code_copies + one_copies:
        copy.wait_recv()
    mine = first_and_last(source)
    two_copies = []
    for n, (d, dk) in enumerate(OFFSETS):
        for part, (group, stage, got, parents, home) in enumerate((
                (x_group, stage_a, got_a, held_a, x), (y_group, stage_b, got_b, held_b, y))):
            if n == 0:
                pair = mine
            else:
                back = OFFSETS.index(((4 - d) % 4, dk))
                row = back - 1 if part == 0 or d == 0 else 7 + back - 2
                pair = first_and_last([codes[row, 0, 0, j] for j in range(4)])
            for s, code in enumerate(pair):
                parent = (code >> 6) & 3 if part == 0 else (code >> 4) & 3
                value = parents[(home - parent + 4) & 3, code & 7]
                if n == 0:
                    got[0, s] = value
                else:
                    stage[n, s] = value
            if n:
                two_copies.append(send(stage.at[n], got.at[n], two_send.at[part, n],
                                       two_recv.at[part, n], (group[n], col)))
    ring_step(3)
    ring_step(4)

    for copy in two_copies:
        copy.wait_recv()
    for s, code in enumerate(mine):
        core = ((code >> 3) & 1) ^ k
        picked_a[s] = got_a[((y - ((code >> 4) & 3) + 4) & 3) * 2 + core, s]
        picked_b[s] = got_b[((x - ((code >> 6) & 3) + 4) & 3) * 2 + core, s]
    refine(picked_a, picked_b, spread, left)
    for t in range(4):
        cols = slice(256 * t, 256 * t + 256)
        fresh[:, cols] = jnp.dot(left[...], children[:, cols], preferred_element_type=F32)
    keep = [1 - refined[j] for j in range(4)]
    keep[0] = jnp.where(moved[0, 0] > 0, 0, keep[0])
    kept = by_slot(lane_ids(8), keep) == 1

    def merge(t, carry):
        cols = pl.ds(pl.multiple_of(128 * t, 128), 128)
        for p in range(NPOP):
            for rt in range(2):
                rows = slice(16 * p + 8 * rt, 16 * p + 8 * rt + 8)
                fresh[rows, cols] = jnp.where(
                    kept, held[p, 8 * rt:8 * rt + 8, cols],
                    fresh[rows, cols])
        return carry

    lax.fori_loop(0, 8, merge, 0)

    for way in range(2):
        for s in range(len(SPLITS)):
            ring[way * STEPS + STEPS - 1, s].wait_recv()
    for h in range(2):
        left[:, 128 * h:128 * h + 128] = landing[table[1 + h, entry]].reshape(NPOP * LX, 128)
    for t in range(4):
        cols = slice(256 * t, 256 * t + 256)
        fresh[:, cols] += jnp.dot(left[...], trades[:, cols], preferred_element_type=F32)

    def trade_faces(turn, moves, first):
        return [send(a, b, halo_send.at[turn, first + n], halo_recv.at[turn, first + n],
                     (near_row[sx], near_col[sy])) for n, (a, b, sx, sy) in enumerate(moves)]

    def step(turn, compute, field, base, lead, faces, arrivals):
        (xs, ys, cs), (xr, yr, cr) = faces, arrivals
        lax.fori_loop(0, 2, lambda n, c: compute(7 - 7 * n, c), 0)
        y_faces(field, ys, cs, base, lead)
        moves = [(cs.at[n], cr.at[n], sx, sy) for n, (p, sx, sy) in enumerate(CORNERS)]
        moves += [(ys.at[0], yr.at[0], 0, 1), (ys.at[1], yr.at[1], 0, -1)]
        copies = trade_faces(turn, moves, 0)
        lax.fori_loop(1, 7, compute, 0)
        x_faces(field, xs, base, lead)
        return copies + trade_faces(
            turn, [(xs.at[0], xr.at[0], 1, 0), (xs.at[1], xr.at[1], -1, 0)], 6)

    def first_step(t, carry):
        cols = pl.ds(pl.multiple_of(128 * t, 128), 128)
        wide_cols = pl.ds(pl.multiple_of(128 * t + 128, 128), 128)
        for rt in range(2):
            f = [fresh[16 * p + 8 * rt:16 * p + 8 * rt + 8, cols] for p in range(NPOP)]
            for p, value in enumerate(collide(f)):
                wide[p, 8 + 8 * rt:16 + 8 * rt, wide_cols] = value
        return carry

    def second_step(t, carry):
        cols = pl.ds(pl.multiple_of(128 * t, 128), 128)
        for rt in range(2):
            f = [pulled(wide, p, rt, t) for p in range(NPOP)]
            for p, value in enumerate(collide(f)):
                relaxed[p, 8 * rt:8 * rt + 8, cols] = value
        return carry

    arrivals = (xr1, yr1, cr1)
    for copy in step(0, first_step, wide, 8, 128, (xs1, ys1, cs1), arrivals):
        copy.wait_recv()
    fill_edges(xr1, yr1, cr1, wide)
    copies = step(1, second_step, relaxed, 0, 0, (xs2, ys2, cs2), (xr2, yr2, cr2))
    store = pltpu.make_async_copy(relaxed, relaxed_out, local.at[6])
    store.start()
    for copy in copies:
        copy.wait_recv()
    for copy in pending:
        copy.wait_send()
    store.wait()


FINAL_GROUPS = ((0, 7), (7, 11), (11, 15), (15, 19), (19, 26))


def final_kernel(relaxed, xr, yr, cr, out_flow, out_heat, wide, result, load, store):
    loads = []
    for n, (lo, hi) in enumerate(FINAL_GROUPS):
        copy = pltpu.make_async_copy(relaxed.at[lo:hi],
                                     wide.at[lo:hi, 8:24, 128:128 + LANES], load.at[n])
        copy.start()
        loads.append(copy)
    fill_edges(xr, yr, cr, wide)
    stores = []
    for n, (lo, hi) in enumerate(FINAL_GROUPS):
        loads[n].wait()

        for p in range(lo, hi):
            for rt in range(2):
                for t in range(8):
                    result[p, 8 * rt:8 * rt + 8, 128 * t:128 * t + 128] = pulled(wide, p, rt, t)
        target = out_flow.at[lo:hi] if hi <= 19 else out_heat
        copy = pltpu.make_async_copy(result.at[lo:hi], target, store.at[n])
        copy.start()
        stores.append(copy)
    for copy in stores:
        copy.wait()


VMEM = pl.BlockSpec(memory_space=pltpu.VMEM)
SMEM = pl.BlockSpec(memory_space=pltpu.SMEM)
ANY = pl.BlockSpec(memory_space=pl.ANY)


def struct(shape, dtype=F32):
    return jax.ShapeDtypeStruct(shape, dtype)


FACES = [struct((2, 8, LANES)), struct((2, 3, LX, 128)), struct((4, 8, 128))]
FIELD = struct((NPOP, LX, LANES))
WIDE = pltpu.VMEM((NPOP, 32, LANES + 256), F32)


def call(kernel, ins, outs, places, scratch, **params):
    return pl.pallas_call(
        kernel, out_shape=outs, in_specs=ins, out_specs=places, scratch_shapes=scratch,
        compiler_params=pltpu.CompilerParams(vmem_limit_bytes=56 * 2**20, **params))


def vmem(spec):
    return pltpu.VMEM(spec.shape, spec.dtype)


def per_device(held_flow, held_heat, coarse_flow, coarse_heat, pair_mask, moved_count, refine_src):
    dma = pltpu.SemaphoreType.DMA
    ns = len(SPLITS)
    slots = 2 * STEPS
    field = pltpu.VMEM((NPOP, LX, LANES), F32)
    block = (NPOP, LX, 128)
    relaxed, *faces = call(
        main_kernel, [SMEM] * 4 + [ANY] * 4, [FIELD] + FACES, [ANY] + [VMEM] * 3,
        [field, pltpu.VMEM((19, 4096), BF16), pltpu.VMEM((7, 4096), BF16), field,
         pltpu.VMEM((2,) + block, BF16), pltpu.VMEM((slots,) + block, BF16),
         pltpu.VMEM((slots,) + block, BF16),
         pltpu.VMEM((4, 8, ROWS_A, 128), BF16), pltpu.VMEM((4, 8, ROWS_B, 128), BF16),
         pltpu.SMEM((13, 1, 1, 4), jnp.int32),
         pltpu.VMEM((8, 2, ROWS_A, 128), BF16), pltpu.VMEM((8, 2, ROWS_B, 128), BF16),
         pltpu.VMEM((8, 2, ROWS_A, 128), BF16), pltpu.VMEM((8, 2, ROWS_B, 128), BF16),
         pltpu.VMEM((2, ROWS_A, 128), BF16), pltpu.VMEM((2, ROWS_B, 128), BF16),
         pltpu.VMEM((NPOP * 32, 128), F32), pltpu.VMEM((NPOP * LX, 256), BF16),
         pltpu.VMEM((256, LANES), BF16), pltpu.VMEM((256, LANES), BF16),
         pltpu.VMEM((NPOP * LX, LANES), F32), WIDE]
        + [vmem(f) for f in FACES * 3]
        + [dma((slots, ns)), dma((slots, ns)), dma((13,)), dma((13,)),
           dma((2, 4)), dma((2, 4)), dma((2, 8)), dma((2, 8)), dma((2, 8)), dma((2, 8)), dma((7,))],
        collective_id=0, has_side_effects=True)(
            jnp.asarray(RING_TABLE), pair_mask, moved_count, refine_src,
            held_flow, held_heat, coarse_flow.reshape(19, 4096), coarse_heat.reshape(7, 4096))
    groups = len(FINAL_GROUPS)
    return tuple(call(
        final_kernel, [ANY] + [VMEM] * 3, [struct((19, LX, LANES)), struct((7, LX, LANES))],
        [ANY] * 2, [WIDE, field, dma((groups,)), dma((groups,))])(relaxed, *faces))


def solution(mesh):
    return jax.shard_map(
        per_device,
        mesh=mesh,
        in_specs=(
            P(None, "brow", "bcol"),
            P(None, "brow", "bcol"),
            P(None, "brow", "bcol", None),
            P(None, "brow", "bcol", None),
            P("brow"),
            P("brow", "bcol"),
            P("brow", "bcol", None),
        ),
        out_specs=(P(None, "brow", "bcol"), P(None, "brow", "bcol")),
        check_vma=False,
    )
```

```python
import jax
import jax.numpy as jnp
import numpy as np
from jax import lax
from jax.experimental import pallas as pl
from jax.experimental.pallas import tpu as pltpu
from jax.sharding import PartitionSpec as P

MESH = pl.DeviceIdType.MESH
F32 = jnp.float32
BF16 = jnp.bfloat16

NPOP = 26
LX = 16
LANES = 1024
RING = 16
JUMPS = (1, 2, 2, 2, 1)
STEPS = len(JUMPS)
SPLITS = ((0, 9), (9, 18), (18, 26))
ROWS_A, ROWS_B = 64, 48

flow_cx = [0, 1, -1, 0, 0, 0, 0, 1, -1, 1, -1, 1, -1, 1, -1, 0, 0, 0, 0]
flow_cy = [0, 0, 0, 1, -1, 0, 0, 1, -1, -1, 1, 0, 0, 0, 0, 1, -1, 1, -1]
flow_cz = [0, 0, 0, 0, 0, 1, -1, 0, 0, 0, 0, 1, -1, -1, 1, 1, -1, -1, 1]
flow_weight = [1.0 / 3.0] + [1.0 / 18.0] * 6 + [1.0 / 36.0] * 12
flow_reverse = [0, 2, 1, 4, 3, 6, 5, 8, 7, 10, 9, 12, 11, 14, 13, 16, 15, 18, 17]
heat_reverse = [0, 2, 1, 4, 3, 6, 5]
POP_CX = flow_cx + flow_cx[:7]
POP_CY = flow_cy + flow_cy[:7]
POP_CZ = flow_cz + flow_cz[:7]
POP_REV = flow_reverse + [19 + r for r in heat_reverse]
X_UP = [i for i in range(NPOP) if POP_CX[i] == 1]
X_DOWN = [i for i in range(NPOP) if POP_CX[i] == -1]
Y_UP = [i for i in range(NPOP) if POP_CY[i] == 1]
Y_DOWN = [i for i in range(NPOP) if POP_CY[i] == -1]
CORNERS = ((7, 1, 1), (8, -1, -1), (9, 1, -1), (10, -1, 1))
tau_flow = 0.8
tau_heat = 0.7
tau_flow_coarse = 0.65
tau_heat_coarse = 0.6
buoyancy = 0.01
heat_ref = 7.0


def ring_plan(mask):
    travels = {d: [] for d in range(RING // 2 + 1)}
    for picks in range(1 << STEPS):
        steps = tuple(t for t in range(STEPS) if picks >> t & 1)
        travels.setdefault(sum(JUMPS[t] for t in steps), []).append(steps)
    for d in travels:
        travels[d].sort(key=lambda steps: (len(steps), steps))
    packets = []
    for c in range(RING):
        d = ((c ^ mask) - c) % RING
        for h in range(2):
            way = h if 2 * d == RING else int(2 * d > RING)
            packets.append((c, h, way, travels[min(d, RING - d)]))
    used = set()
    plan = {}

    def copies(c, way, steps):
        out = []
        for t in steps:
            out.append((way, t, c))
            c = (c + (1 - 2 * way) * JUMPS[t]) % RING
        return out

    def place(left):
        if not left:
            return True
        fits = [[steps for steps in p[3] if used.isdisjoint(copies(p[0], p[2], steps))]
                for p in left]
        n = min(range(len(left)), key=lambda i: len(fits[i]))
        c, h, way, _ = left[n]
        for steps in fits[n]:
            taken = copies(c, way, steps)
            used.update(taken)
            plan[c, h] = (way, steps, taken)
            if place(left[:n] + left[n + 1:]):
                return True
            used.difference_update(taken)
        return False

    assert place(packets)
    return plan


def ring_tables():
    code = np.zeros((RING, RING, 2 * STEPS), np.int32)
    land = np.zeros((2, RING, RING), np.int32)
    for mask in range(1, RING):
        for (c, h), (way, steps, taken) in ring_plan(mask).items():
            source = h
            for _, t, node in taken:
                code[mask, node, way * STEPS + t] = source
                source = 2 + t
            land[h, mask, c ^ mask] = way * STEPS + steps[-1]
    word = sum(code[:, :, n] << (3 * n) for n in range(2 * STEPS))
    kinds = [sorted(set(code[:, :, n].reshape(-1).tolist())) for n in range(2 * STEPS)]
    return np.stack([word.reshape(-1), land[0].reshape(-1), land[1].reshape(-1)]), kinds


RING_TABLE, RING_KINDS = ring_tables()


def lane_ids(rows):
    return lax.broadcasted_iota(jnp.int32, (rows, 128), 1)


def total(values):
    values = list(values)
    while len(values) > 1:
        values = [a + b for a, b in zip(values[::2], values[1::2])] + (
            [values[-1]] if len(values) % 2 else [])
    return values[0]


def moments(f, push):
    rho = total(f[:19])
    heat = total(f[19:])

    def along(c):
        ups = [f[i] for i in range(19) if c[i] == 1]
        downs = [f[i] for i in range(19) if c[i] == -1]
        return total([u - d for u, d in zip(ups, downs)])

    mx, my, mz = along(flow_cx), along(flow_cy), along(flow_cz)
    force = None
    if push:
        force = buoyancy * rho * (heat - heat_ref)
        mz = mz + 0.5 * force
    inv = 1.0 / rho
    return rho, heat, force, (mx, my, mz), (mx * inv, my * inv, mz * inv)


def dot_dir(i, v):
    terms = []
    for c, a in zip((flow_cx[i], flow_cy[i], flow_cz[i]), v):
        if c:
            terms.append((c, a))
    out = terms[0][1] if terms[0][0] > 0 else -terms[0][1]
    for c, a in terms[1:]:
        out = out + a if c > 0 else out - a
    return out


PAIRS = [(1, 2), (3, 4), (5, 6), (7, 8), (9, 10), (11, 12), (13, 14), (15, 16), (17, 18)]


def collide(f):
    rho, heat, force, mom, vel = moments(f, True)
    rate = 1.0 / tau_flow
    keep = 1.0 - rate
    gain = 1.0 - 0.5 / tau_flow
    speed = mom[0] * vel[0] + mom[1] * vel[1] + mom[2] * vel[2]
    common = rate * rho - (1.5 * rate) * speed - (3.0 * gain) * force * vel[2]
    fgain = (9.0 * gain) * force
    fodd = (3.0 * gain) * force
    out = [None] * NPOP
    out[0] = keep * f[0] + flow_weight[0] * common
    for i, j in PAIRS:
        w = flow_weight[i]
        cu = dot_dir(i, vel)
        cm = dot_dir(i, mom)
        bracket = (4.5 * rate) * cm
        odd = (3.0 * rate) * cm
        if flow_cz[i] == 1:
            bracket = bracket + fgain
            odd = odd + fodd
        elif flow_cz[i] == -1:
            bracket = bracket - fgain
            odd = odd - fodd
        even = common + bracket * cu
        out[i] = keep * f[i] + w * (even + odd)
        out[j] = keep * f[j] + w * (even - odd)
    hrate = 1.0 / tau_heat
    hkeep = 1.0 - hrate
    out[19] = hkeep * f[19] + (0.25 * hrate) * heat
    side = (0.125 * hrate) * heat
    for k, a in zip((20, 22, 24), vel):
        tilt = 4.0 * side * a
        out[k] = hkeep * f[k] + (side + tilt)
        out[k + 1] = hkeep * f[k + 1] + (side - tilt)
    return out


def explode(f):
    rho, heat, _, mom, vel = moments(f, False)
    blend = tau_flow / (2.0 * tau_flow_coarse)
    rest = 1.0 - blend
    speed = mom[0] * vel[0] + mom[1] * vel[1] + mom[2] * vel[2]
    common = rest * rho - (1.5 * rest) * speed
    out = [None] * NPOP
    out[0] = blend * f[0] + flow_weight[0] * common
    for i, j in PAIRS:
        w = flow_weight[i]
        cu = dot_dir(i, vel)
        cm = dot_dir(i, mom)
        even = common + ((4.5 * rest) * cm) * cu
        odd = (3.0 * rest) * cm
        out[i] = blend * f[i] + w * (even + odd)
        out[j] = blend * f[j] + w * (even - odd)
    hblend = tau_heat / (2.0 * tau_heat_coarse)
    hrest = 1.0 - hblend
    out[19] = hblend * f[19] + (0.25 * hrest) * heat
    side = (0.125 * hrest) * heat
    for k, a in zip((20, 22, 24), vel):
        tilt = 4.0 * side * a
        out[k] = hblend * f[k] + (side + tilt)
        out[k + 1] = hblend * f[k + 1] + (side - tilt)
    return out


def pack_trade(held, own, lo, hi):
    group = lane_ids(LX) % 64 // 16
    for p in range(lo, hi):
        for q in range(2):
            packed = held[p, :, 512 * q:512 * q + 128]
            for kk in range(1, 4):
                k = 4 * q + kk
                tile = held[p, :, 128 * k:128 * k + 128]
                packed = jnp.where(group == kk, pltpu.roll(tile, 16 * kk, 1), packed)
            own[q, p] = packed.astype(BF16)


def pack_coarse(cf, ch, spread, put):
    for t in range(32):
        cols = slice(128 * t, 128 * t + 128)
        flow = cf[:, cols].astype(F32)
        heat = ch[:, cols].astype(F32)
        spread[pl.ds(t, 8, stride=32), :] = flow[0:8]
        spread[pl.ds(8 * 32 + t, 8, stride=32), :] = flow[8:16]
        spread[pl.ds(16 * 32 + t, 3, stride=32), :] = flow[16:19]
        spread[pl.ds(19 * 32 + t, 7, stride=32), :] = heat
    high = lane_ids(8) // 8 % 2 == 1
    zeros = jnp.zeros((8, 128), F32)
    for ox in range(2):
        for oy in range(2):
            low_rows, high_rows = [], []
            for pair in range(13):
                a = spread[pl.ds(pair * 32 + 16 * ox + oy, 8, stride=2), :]
                b = spread[pl.ds((pair + 13) * 32 + 16 * ox + oy, 8, stride=2), :]
                low_rows.append(jnp.where(high, pltpu.roll(b, 8, 1), a))
                high_rows.append(jnp.where(high, b, pltpu.roll(a, 120, 1)))
            for oz, rows in ((0, low_rows), (1, high_rows)):
                rows = rows + [zeros]
                for i in range(7):
                    put(4 * ox + 2 * oy + oz, i,
                        jnp.concatenate([rows[2 * i], rows[2 * i + 1]], axis=0).astype(BF16))


def place():
    me = lax.axis_index("brow")
    col = lax.axis_index("bcol")
    return me // 8, me // 2 % 4, me % 2, col


def row_of(x, y, k):
    return (x * 4 + y) * 2 + k


OFFSETS = [(d, dk) for d in range(4) for dk in range(2)]


OFFSETS = [(d, dk) for d in range(4) for dk in range(2)]


def x_faces(field, xs, base, lead):
    for n, p in enumerate(X_UP):
        xs[0, n:n + 1, :] = field[p, base + 15:base + 16, lead:lead + LANES]
    for n, p in enumerate(X_DOWN):
        xs[1, n:n + 1, :] = field[p, base:base + 1, lead:lead + LANES]


def y_faces(field, ys, cs, base, lead):
    low = lane_ids(LX) < 64
    rows = slice(base, base + LX)
    last = slice(lead + LANES - 128, lead + LANES)
    first = slice(lead, lead + 128)
    for n, (p, sx, sy) in enumerate(CORNERS):
        top = base + 8 if sx == 1 else base
        cs[n] = field[p, top:top + 8, last if sy == 1 else first]
    for n in range(3):
        a, b = Y_UP[2 * n], Y_UP[2 * n + 1]
        ys[0, n] = jnp.where(low, pltpu.roll(field[a, rows, last], 64, 1), field[b, rows, last])
        a, b = Y_DOWN[2 * n], Y_DOWN[2 * n + 1]
        ys[1, n] = jnp.where(low, field[a, rows, first], pltpu.roll(field[b, rows, first], 64, 1))


def fill_edges(xr, yr, cr, wide):
    for n, (p, sx, sy) in enumerate(CORNERS):
        rows = slice(0, 8) if sx == 1 else slice(24, 32)
        cols = slice(0, 128) if sy == 1 else slice(128 + LANES, 256 + LANES)
        wide[p, rows, cols] = cr[n]
    for n, p in enumerate(X_UP):
        wide[p, 7:8, 128:128 + LANES] = xr[0, n:n + 1, :]
    for n, p in enumerate(X_DOWN):
        wide[p, 24:25, 128:128 + LANES] = xr[1, n:n + 1, :]
    for n in range(3):
        a, b = Y_UP[2 * n], Y_UP[2 * n + 1]
        wide[a, 8:24, 0:128] = pltpu.roll(yr[0, n], 64, 1)
        wide[b, 8:24, 0:128] = yr[0, n]
        a, b = Y_DOWN[2 * n], Y_DOWN[2 * n + 1]
        wide[a, 8:24, 128 + LANES:256 + LANES] = yr[1, n]
        wide[b, 8:24, 128 + LANES:256 + LANES] = pltpu.roll(yr[1, n], 64, 1)


def pulled(wide, p, rt, k):
    cx, cy, cz = POP_CX[p], POP_CY[p], POP_CZ[p]
    rows = slice(8 + 8 * rt - cx, 16 + 8 * rt - cx)

    def tile(e):
        if isinstance(e, int):
            return slice(128 * e, 128 * e + 128)
        return pl.ds(pl.multiple_of(128 * e, 128), 128)

    low = lane_ids(8) < 64
    value = wide[p, rows, tile(k + 1)]
    shift = 0
    if cy == 1:
        value = jnp.where(low, value, wide[p, rows, tile(k)])
        shift = 64
    elif cy == -1:
        value = jnp.where(low, wide[p, rows, tile(k + 2)], value)
        shift = 64
    shift = (shift + cz) % 128
    if shift:
        value = pltpu.roll(value, shift, 1)
    if cz:
        wall = lane_ids(8) % 64 == (0 if cz == 1 else 63)
        back = wide[POP_REV[p], 8 + 8 * rt:16 + 8 * rt, tile(k + 1)]
        value = jnp.where(wall, back, value)
    return value


def by_slot(lane, picks):
    slot = lane % 64 // 16
    return jnp.where(slot == 0, picks[0], jnp.where(
        slot == 1, picks[1], jnp.where(slot == 2, picks[2], picks[3])))


def first_and_last(values):
    first, last = values[3], values[0]
    for j in (2, 1, 0):
        first = jnp.where(values[j] >= 0, values[j], first)
    for j in (1, 2, 3):
        last = jnp.where(values[j] >= 0, values[j], last)
    return first, last


def one_hots(children, trades, child, trade):
    for t in range(8):
        lane = lax.broadcasted_iota(jnp.int32, (1, 128), 1)
        yy = 2 * t + lane // 64
        want = yy // 2 * 16 + lane % 16 // 2 + by_slot(lane, child)
        row = lax.broadcasted_iota(jnp.int32, (128, 128), 0)
        hot = jnp.where(row == want, 1.0, 0.0).astype(BF16)
        cols = slice(128 * t, 128 * t + 128)
        children[0:128, cols] = hot
        children[128:256, cols] = hot
        row = lax.broadcasted_iota(jnp.int32, (256, 128), 0)
        z = lane % 64
        want = yy // 8 * 128 + yy % 2 * 64 + yy % 8 // 2 * 16 + z
        want = jnp.where(z < 16, want + trade, 1 << 20)
        trades[:, cols] = jnp.where(row == want, 1.0, 0.0).astype(BF16)


def refine(picked_a, picked_b, spread, left):
    high = lane_ids(8) // 8 % 2 == 1
    values = [None] * NPOP
    for pair in range(13):
        part, row = (picked_a, 8 * pair) if pair < 8 else (picked_b, 8 * pair - 64)
        base = row // 16 * 16
        a = part[0, base:base + 16, :].astype(F32)[row - base:row - base + 8]
        b = part[1, base:base + 16, :].astype(F32)[row - base:row - base + 8]
        values[pair] = jnp.where(high, pltpu.roll(b, 8, 1), a)
        values[pair + 13] = jnp.where(high, b, pltpu.roll(a, 120, 1))
    for p, value in enumerate(explode(values)):
        spread[pl.ds(16 * p, 8, stride=2), :] = value
        spread[pl.ds(16 * p + 1, 8, stride=2), :] = value
    for p in range(NPOP):
        rows = slice(16 * p, 16 * p + 16)
        value = spread[rows, :]
        top = value.astype(BF16)
        left[rows, 0:128] = top
        left[rows, 128:256] = (value - top.astype(F32)).astype(BF16)


def main_kernel(table_in, mask_in, moved_in, codes_all, hf, hh, cf, ch,
                relaxed_out, xr2, yr2, cr2,
                table, mask_ref, moved, codes_in, held, cfv, chv, relaxed, own, landing, leaving, held_a, held_b, codes,
                stage_a, stage_b, got_a, got_b, picked_a, picked_b,
                spread, left, children, trades, fresh, wide,
                xs1, ys1, cs1, xr1, yr1, cr1, xs2, ys2, cs2,
                ring_send, ring_recv, code_send, code_recv, one_send, one_recv,
                two_send, two_recv, halo_send, halo_recv, local):
    x, y, k, col = place()
    me = row_of(x, y, k)
    x_group = [row_of(x, (y + d) % 4, (k + dk) % 2) for d, dk in OFFSETS]
    y_group = [row_of((x + d) % 4, y, (k + dk) % 2) for d, dk in OFFSETS]
    peers = x_group[1:] + y_group[2:]
    near_row = {1: (me + 1) % 32, -1: (me + 31) % 32, 0: me}
    near_col = {d: (col + d + RING) % RING for d in (-2, -1, 0, 1, 2)}

    barrier = pltpu.get_barrier_semaphore()
    greeted = [(me, near_col[d]) for d in (-2, -1, 1, 2)] + [(peer, col) for peer in peers]
    greeted += [(near_row[sx], near_col[sy]) for sx in (-1, 1) for sy in (-1, 0, 1)]
    for device in reversed(greeted):
        pl.semaphore_signal(barrier, inc=1, device_id=device, device_id_type=MESH)

    def load(source, target, n):
        copy = pltpu.make_async_copy(source, target, local.at[n])
        copy.start()
        return copy

    scalars = [load(table_in, table, 7), load(mask_in, mask_ref, 8),
               load(moved_in, moved, 9), load(codes_all, codes_in, 10)]
    loads = [[load(hf.at[0:9], held.at[0:9], 0)],
             [load(hf.at[9:18], held.at[9:18], 1)],
             [load(hf.at[18:19], held.at[18:19], 2), load(hh, held.at[19:26], 3)],
             [load(cf, cfv, 4), load(ch, chv, 5)]]

    pending = []

    def send(source, target, sends, recvs, device):
        copy = pltpu.make_async_remote_copy(
            src_ref=source, dst_ref=target, send_sem=sends, recv_sem=recvs,
            device_id=device, device_id_type=MESH)
        copy.start()
        pending.append(copy)
        return copy

    for copy in scalars:
        copy.wait()
    entry = mask_ref[0] * RING + col
    word = table[0, entry]
    ring = {}

    def ring_send_of(step, s):
        lo, hi = SPLITS[s]
        for way in range(2):
            slot = way * STEPS + step
            code = (word >> (3 * slot)) & 7
            if step:
                ring[slot - 1, s].wait_recv()
            value = own[0, lo:hi]
            for kind in RING_KINDS[slot]:
                if kind == 1:
                    value = jnp.where(code == 1, own[1, lo:hi], value)
                elif kind:
                    value = jnp.where(code == kind, landing[way * STEPS + kind - 2, lo:hi], value)
            leaving[slot, lo:hi] = value
            ring[slot, s] = send(leaving.at[slot, lo:hi], landing.at[slot, lo:hi],
                                 ring_send.at[slot, s], ring_recv.at[slot, s],
                                 (me, near_col[(1 - 2 * way) * JUMPS[step]]))

    def ring_step(step):
        for s in range(len(SPLITS)):
            ring_send_of(step, s)

    for s, (lo, hi) in enumerate(SPLITS):
        for copy in loads[s]:
            copy.wait()
        pack_trade(held, own, lo, hi)
        if s == 0:
            pl.semaphore_wait(barrier, len(greeted))
        ring_send_of(0, s)
    code_copies = [send(codes_in, codes.at[n], code_send.at[n], code_recv.at[n], (peer, col))
                   for n, peer in enumerate(peers)]

    def put(octant, i, value):
        if i < 4:
            held_a[0, octant, 16 * i:16 * i + 16, :] = value
        else:
            held_b[0, octant, 16 * (i - 4):16 * (i - 4) + 16, :] = value

    for copy in loads[3]:
        copy.wait()
    pack_coarse(cfv, chv, spread, put)
    one_copies = []
    for d in (2, 1, 3):
        one_copies.append(send(held_a.at[0], held_a.at[d], one_send.at[0, d], one_recv.at[0, d],
                               (row_of((x + d) % 4, y, k), col)))
        one_copies.append(send(held_b.at[0], held_b.at[d], one_send.at[1, d], one_recv.at[1, d],
                               (row_of(x, (y + d) % 4, k), col)))
    ring_step(1)

    source = [codes_in[0, 0, j] for j in range(4)]
    refined = [jnp.where(v >= 0, 1, 0) for v in source]
    rank = [0]
    for j in range(3):
        rank.append(rank[-1] + refined[j])
    child = [jnp.where(refined[j] == 1, rank[j] * 8, 1 << 20) for j in range(4)]
    trade = jnp.where((moved[0, 0] > 0) & (refined[0] == 0), 0, 1 << 20)
    one_hots(children, trades, child, trade)
    ring_step(2)

    for copy in code_copies + one_copies:
        copy.wait_recv()
    mine = first_and_last(source)
    two_copies = []
    for n, (d, dk) in enumerate(OFFSETS):
        for part, (group, stage, got, parents, home) in enumerate((
                (x_group, stage_a, got_a, held_a, x), (y_group, stage_b, got_b, held_b, y))):
            if n == 0:
                pair = mine
            else:
                back = OFFSETS.index(((4 - d) % 4, dk))
                row = back - 1 if part == 0 or d == 0 else 7 + back - 2
                pair = first_and_last([codes[row, 0, 0, j] for j in range(4)])
            for s, code in enumerate(pair):
                parent = (code >> 6) & 3 if part == 0 else (code >> 4) & 3
                value = parents[(home - parent + 4) & 3, code & 7]
                if n == 0:
                    got[0, s] = value
                else:
                    stage[n, s] = value
            if n:
                two_copies.append(send(stage.at[n], got.at[n], two_send.at[part, n],
                                       two_recv.at[part, n], (group[n], col)))
    ring_step(3)
    ring_step(4)

    for copy in two_copies:
        copy.wait_recv()
    for s, code in enumerate(mine):
        core = ((code >> 3) & 1) ^ k
        picked_a[s] = got_a[((y - ((code >> 4) & 3) + 4) & 3) * 2 + core, s]
        picked_b[s] = got_b[((x - ((code >> 6) & 3) + 4) & 3) * 2 + core, s]
    refine(picked_a, picked_b, spread, left)
    for t in range(4):
        cols = slice(256 * t, 256 * t + 256)
        fresh[:, cols] = jnp.dot(left[...], children[:, cols], preferred_element_type=F32)
    keep = [1 - refined[j] for j in range(4)]
    keep[0] = jnp.where(moved[0, 0] > 0, 0, keep[0])
    kept = by_slot(lane_ids(8), keep) == 1

    def merge(t, carry):
        cols = pl.ds(pl.multiple_of(128 * t, 128), 128)
        for p in range(NPOP):
            for rt in range(2):
                rows = slice(16 * p + 8 * rt, 16 * p + 8 * rt + 8)
                fresh[rows, cols] = jnp.where(
                    kept, held[p, 8 * rt:8 * rt + 8, cols],
                    fresh[rows, cols])
        return carry

    lax.fori_loop(0, 8, merge, 0)

    for way in range(2):
        for s in range(len(SPLITS)):
            ring[way * STEPS + STEPS - 1, s].wait_recv()
    for h in range(2):
        left[:, 128 * h:128 * h + 128] = landing[table[1 + h, entry]].reshape(NPOP * LX, 128)
    def trade_faces(turn, moves, first):
        return [send(a, b, halo_send.at[turn, first + n], halo_recv.at[turn, first + n],
                     (near_row[sx], near_col[sy])) for n, (a, b, sx, sy) in enumerate(moves)]

    def step(turn, compute, field, base, lead, faces, arrivals):
        (xs, ys, cs), (xr, yr, cr) = faces, arrivals
        compute(7, 0)
        compute(0, 0)
        y_faces(field, ys, cs, base, lead)
        moves = [(cs.at[n], cr.at[n], sx, sy) for n, (p, sx, sy) in enumerate(CORNERS)]
        moves += [(ys.at[0], yr.at[0], 0, 1), (ys.at[1], yr.at[1], 0, -1)]
        copies = trade_faces(turn, moves, 0)
        for t in range(1, 7):
            compute(t, 0)
        x_faces(field, xs, base, lead)
        return copies + trade_faces(
            turn, [(xs.at[0], xr.at[0], 1, 0), (xs.at[1], xr.at[1], -1, 0)], 6)

    def first_step(t, carry):
        cols = slice(128 * t, 128 * t + 128)
        wide_cols = slice(128 * t + 128, 128 * t + 256)
        came = jnp.dot(left[...], trades[:, cols], preferred_element_type=F32)
        for rt in range(2):
            f = [fresh[16 * p + 8 * rt:16 * p + 8 * rt + 8, cols]
                 + came[16 * p + 8 * rt:16 * p + 8 * rt + 8] for p in range(NPOP)]
            for p, value in enumerate(collide(f)):
                wide[p, 8 + 8 * rt:16 + 8 * rt, wide_cols] = value
        return carry

    def second_step(t, carry):
        cols = slice(128 * t, 128 * t + 128)
        for rt in range(2):
            f = [pulled(wide, p, rt, t) for p in range(NPOP)]
            for p, value in enumerate(collide(f)):
                relaxed[p, 8 * rt:8 * rt + 8, cols] = value
        return carry

    arrivals = (xr1, yr1, cr1)
    for copy in step(0, first_step, wide, 8, 128, (xs1, ys1, cs1), arrivals):
        copy.wait_recv()
    fill_edges(xr1, yr1, cr1, wide)
    copies = step(1, second_step, relaxed, 0, 0, (xs2, ys2, cs2), (xr2, yr2, cr2))
    store = pltpu.make_async_copy(relaxed, relaxed_out, local.at[6])
    store.start()
    for copy in copies:
        copy.wait_recv()
    for copy in pending:
        copy.wait_send()
    store.wait()


FINAL_GROUPS = ((0, 7), (7, 11), (11, 15), (15, 19), (19, 26))


def final_kernel(relaxed, xr_in, yr_in, cr_in, out_flow, out_heat,
                 wide, result, xr, yr, cr, load, store):
    faces = []
    for n, (source, target) in enumerate(((xr_in, xr), (yr_in, yr), (cr_in, cr))):
        copy = pltpu.make_async_copy(source, target, load.at[len(FINAL_GROUPS) + n])
        copy.start()
        faces.append(copy)
    loads = []
    for n, (lo, hi) in enumerate(FINAL_GROUPS):
        copy = pltpu.make_async_copy(relaxed.at[lo:hi],
                                     wide.at[lo:hi, 8:24, 128:128 + LANES], load.at[n])
        copy.start()
        loads.append(copy)
    for copy in faces:
        copy.wait()
    fill_edges(xr, yr, cr, wide)
    stores = []
    for n, (lo, hi) in enumerate(FINAL_GROUPS):
        loads[n].wait()

        for p in range(lo, hi):
            for rt in range(2):
                for t in range(8):
                    result[p, 8 * rt:8 * rt + 8, 128 * t:128 * t + 128] = pulled(wide, p, rt, t)
        target = out_flow.at[lo:hi] if hi <= 19 else out_heat
        copy = pltpu.make_async_copy(result.at[lo:hi], target, store.at[n])
        copy.start()
        stores.append(copy)
    for copy in stores:
        copy.wait()


ANY = pl.BlockSpec(memory_space=pl.ANY)
HBM = pl.BlockSpec(memory_space=pltpu.HBM)


def struct(shape, dtype=F32):
    return jax.ShapeDtypeStruct(shape, dtype)


FACES = [struct((2, 8, LANES)), struct((2, 3, LX, 128)), struct((4, 8, 128))]
FIELD = struct((NPOP, LX, LANES))
WIDE = pltpu.VMEM((NPOP, 32, LANES + 256), F32)


def call(kernel, ins, outs, places, scratch, **params):
    return pl.pallas_call(
        kernel, out_shape=outs, in_specs=ins, out_specs=places, scratch_shapes=scratch,
        compiler_params=pltpu.CompilerParams(vmem_limit_bytes=56 * 2**20, **params))


def vmem(spec):
    return pltpu.VMEM(spec.shape, spec.dtype)


def per_device(held_flow, held_heat, coarse_flow, coarse_heat, pair_mask, moved_count, refine_src):
    dma = pltpu.SemaphoreType.DMA
    ns = len(SPLITS)
    slots = 2 * STEPS
    field = pltpu.VMEM((NPOP, LX, LANES), F32)
    block = (NPOP, LX, 128)
    relaxed, *faces = call(
        main_kernel, [HBM] * 4 + [ANY] * 4, [FIELD] + FACES, [ANY] * 4,
        [pltpu.SMEM((3, RING * RING), jnp.int32), pltpu.SMEM((1,), jnp.int32),
         pltpu.SMEM((1, 1), jnp.int32), pltpu.SMEM((1, 1, 4), jnp.int32), field, pltpu.VMEM((19, 4096), BF16), pltpu.VMEM((7, 4096), BF16), field,
         pltpu.VMEM((2,) + block, BF16), pltpu.VMEM((slots,) + block, BF16),
         pltpu.VMEM((slots,) + block, BF16),
         pltpu.VMEM((4, 8, ROWS_A, 128), BF16), pltpu.VMEM((4, 8, ROWS_B, 128), BF16),
         pltpu.SMEM((13, 1, 1, 4), jnp.int32),
         pltpu.VMEM((8, 2, ROWS_A, 128), BF16), pltpu.VMEM((8, 2, ROWS_B, 128), BF16),
         pltpu.VMEM((8, 2, ROWS_A, 128), BF16), pltpu.VMEM((8, 2, ROWS_B, 128), BF16),
         pltpu.VMEM((2, ROWS_A, 128), BF16), pltpu.VMEM((2, ROWS_B, 128), BF16),
         pltpu.VMEM((NPOP * 32, 128), F32), pltpu.VMEM((NPOP * LX, 256), BF16),
         pltpu.VMEM((256, LANES), BF16), pltpu.VMEM((256, LANES), BF16),
         pltpu.VMEM((NPOP * LX, LANES), F32), WIDE]
        + [vmem(f) for f in FACES * 3]
        + [dma((slots, ns)), dma((slots, ns)), dma((13,)), dma((13,)),
           dma((2, 4)), dma((2, 4)), dma((2, 8)), dma((2, 8)), dma((2, 8)), dma((2, 8)), dma((11,))],
        collective_id=0, has_side_effects=True)(
            jnp.asarray(RING_TABLE), pair_mask, moved_count, refine_src,
            held_flow, held_heat, coarse_flow.reshape(19, 4096), coarse_heat.reshape(7, 4096))
    groups = len(FINAL_GROUPS)
    return tuple(call(
        final_kernel, [ANY] * 4, [struct((19, LX, LANES)), struct((7, LX, LANES))],
        [ANY] * 2, [WIDE, field] + [vmem(f) for f in FACES] + [dma((groups + 3,)), dma((groups,))])(relaxed, *faces))


def solution(mesh):
    return jax.shard_map(
        per_device,
        mesh=mesh,
        in_specs=(
            P(None, "brow", "bcol"),
            P(None, "brow", "bcol"),
            P(None, "brow", "bcol", None),
            P(None, "brow", "bcol", None),
            P("brow"),
            P("brow", "bcol"),
            P("brow", "bcol", None),
        ),
        out_specs=(P(None, "brow", "bcol"), P(None, "brow", "bcol")),
        check_vma=False,
    )
```
